32 devices in a mesh: tm: 16 (over z, x, core), space: 2 (over y).
Axes of the slice: x: 2, y: 2, z: 4, core: 2. Of those that a mesh axis runs over, the one named last changes fastest.
Arguments:
- snapshots: bfloat16 [512, 5, 4096], P('tm', None, 'space'), may hold values from -210 to 210, as said below
- basis: bfloat16 [2, 33, 16, 5, 4096], P(None, None, None, None, ('space', 'tm')), may hold values from -6 to 6
- mass_table: float32 [8, 64, 64], replicated, may hold values from -0.03 to 3, as said below
- elem_kind: int32 [64], P(('space', 'tm')), may hold values from 0 to 7
- offsets: int32 [8], replicated, may hold values from 0 to 256, as said below
Outputs:
- coeffs: float32 [2, 33, 8, 16], replicated
- new_basis: bfloat16 [2, 33, 16, 5, 4096], P(None, None, None, None, ('space', 'tm'))
The draws below stay inside these ranges and needn't reach their ends.
Inputs may be any that keep to these rules, and one draw needn't show every extreme that they name: `snapshots`: rows of flow data. `mass_table`: each block is symmetric and positive definite. `offsets`: some block starts at 0 and some at 256.
All inputs are finite; a program needn't handle non-finite values.
Results may differ from the reference program's by a relative error of at most 0.0095.
Values may be sent and summed in bfloat16 or wider, within the bound.
A program may use at most 64 MiB of HBM per device.

```python
import math
import jax
import jax.numpy as jnp
from jax import lax

NVAR = 5
NT = 256
F = 33
RANK = 16
ELEM_PTS = 64
KINDS = 8
RECORD = 512
NB = 8
PD = 128
NPTS = 4096
ELEMS = 64
N_TM = 16
N_SPACE = 2


def draw_snapshots(key, part):
    key_noise, key_scale = jax.random.split(key, 2)
    point_idx = jnp.arange(NPTS, dtype=jnp.int32)
    tm_pos = (point_idx // PD % N_TM).astype(jnp.float32) / max(N_TM - 1, 1)
    space_pos = (point_idx // (PD * N_TM)).astype(jnp.float32) / max(N_SPACE - 1, 1)
    noise = jax.random.normal(key_noise, (RECORD, NVAR, NPTS), jnp.float32)
    ramp = 1.0 + 1.2 * tm_pos + 0.6 * space_pos
    noise = jnp.clip(noise, -6.0, 6.0)
    spread = jnp.exp(jax.random.uniform(key_scale, (1, NVAR, NPTS), jnp.float32, 0.0, math.log(10.0)))
    return (noise * spread * ramp[None, None, :]).astype(jnp.bfloat16)


def draw_mass_table(key, part):
    key_diag, key_off = jax.random.split(key)
    diagonal = jax.random.uniform(key_diag, (KINDS, ELEM_PTS), jnp.float32, 2.0, 3.0)
    off_part = jax.random.uniform(key_off, (KINDS, ELEM_PTS, ELEM_PTS), jnp.float32, -0.03, 0.03)
    symmetric = 0.5 * (off_part + jnp.swapaxes(off_part, 1, 2))
    position = jnp.arange(ELEM_PTS, dtype=jnp.int32)
    on_diag = position[:, None] == position[None, :]
    return jnp.where(on_diag[None], diagonal[:, :, None], symmetric)


def draw_offsets(key, part):
    key_vals, key_perm = jax.random.split(key)
    values = jax.random.randint(key_vals, (NB,), 0, RECORD - NT + 1, dtype=jnp.int32)
    order = jax.random.permutation(key_perm, NB)
    values = values.at[order[0]].set(0)
    values = values.at[order[1]].set(RECORD - NT)
    return values


def plant(values, rng, least, top_value):
    longest = values.shape.index(max(values.shape))
    spots = []
    for shift in (0, 1):
        where = [jax.random.randint(jax.random.fold_in(rng, axis), (), 0, length) for axis, length in enumerate(values.shape)]
        where[longest] = (where[longest] + shift) % values.shape[longest]
        spots.append(tuple(where))
    return values.at[spots[0]].set(least).at[spots[1]].set(top_value)


def shard_levels(own_key, shape, cuts, smallest, high):
    loudness = 1.0
    for dim, shards_of in cuts:
        draws = jax.random.uniform(jax.random.fold_in(jax.random.fold_in(own_key, 6), dim), (shards_of,), jnp.float32, smallest / len(cuts), high / len(cuts))
        loudness = loudness * jnp.repeat(jnp.exp(draws), shape[dim] // shards_of).reshape((-1,) + (1,) * (len(shape) - 1 - dim))
    return loudness


def centred(rng, extent, scale, reach, cuts=(), held_as=jnp.bfloat16):
    gain = shard_levels(rng, extent, cuts, -0.22, 0.18) if cuts else 1.0
    values = jax.random.normal(rng, extent, jnp.float32) * scale * gain
    return jnp.minimum(jnp.maximum(values, -reach), reach).astype(held_as)


def setup_inputs(seed: int = 0) -> dict:
    key_of = jax.random.split(jax.random.key(seed), 6)
    return {
        "snapshots": draw_snapshots(jax.random.fold_in(key_of[5], 71), 0),
        "basis": centred(key_of[1], (2, F, RANK, NVAR, NPTS), 1.0, 6.0, ((4, 32),)),
        "mass_table": draw_mass_table(jax.random.fold_in(key_of[5], 71), 0),
        "elem_kind": plant(jax.random.randint(key_of[3], (ELEMS,), 0, KINDS), jax.random.fold_in(key_of[3], 1), 0, KINDS - 1).astype(jnp.int32),
        "offsets": draw_offsets(jax.random.fold_in(key_of[5], 71), 0),
    }


def spectral_table(offsets, window_len, freq_count, record_len):
    snap_idx = jnp.arange(record_len, dtype=jnp.int32)
    time_lag = snap_idx[None, :] - offsets[:, None].astype(jnp.int32)
    inside = (time_lag >= 0) & (time_lag < window_len)
    lag_clip = jnp.clip(time_lag, 0, window_len - 1)
    lag_float = lag_clip.astype(jnp.float32)
    hann_wt = 0.5 - 0.5 * jnp.cos(2.0 * math.pi / window_len * lag_float)
    norm_wt = 1.0 / math.sqrt(0.375 * window_len)
    freq_idx = jnp.arange(freq_count, dtype=jnp.int32)
    phase_int = jnp.mod(freq_idx[:, None, None] * lag_clip[None], window_len)
    angle = 2.0 * math.pi / window_len * phase_int.astype(jnp.float32)
    weight = jnp.where(inside, hann_wt * norm_wt, jnp.zeros_like(hann_wt))[None]
    real_part = weight * jnp.cos(angle)
    imag_part = -weight * jnp.sin(angle)
    return jnp.stack([real_part, imag_part]).astype(jnp.bfloat16)

def apply_mass(field, mass_blk):
    lead = field.shape[:-1]
    elem_count = mass_blk.shape[0]
    shaped = field.reshape(lead + (elem_count, ELEM_PTS))
    result = jnp.einsum('...ep,epq->...eq', shaped, mass_blk, precision=lax.Precision.HIGHEST)
    return result.reshape(field.shape)

def project(mode_rows, weighted):
    real_out = jnp.einsum('fkx,fbx->fbk', mode_rows[0], weighted[0]) + jnp.einsum('fkx,fbx->fbk', mode_rows[1], weighted[1])
    imag_out = jnp.einsum('fkx,fbx->fbk', mode_rows[0], weighted[1]) - jnp.einsum('fkx,fbx->fbk', mode_rows[1], weighted[0])
    return jnp.stack([real_out, imag_out])

def time_kernel(dft_table, coeffs):
    table_f = dft_table.astype(jnp.float32)
    coeff_round = lax.optimization_barrier(coeffs.astype(jnp.bfloat16)).astype(jnp.float32)
    real_out = jnp.einsum('fbt,fbk->fkt', table_f[0], coeff_round[0]) - jnp.einsum('fbt,fbk->fkt', table_f[1], coeff_round[1])
    imag_out = jnp.einsum('fbt,fbk->fkt', table_f[0], coeff_round[1]) + jnp.einsum('fbt,fbk->fkt', table_f[1], coeff_round[0])
    return jnp.stack([real_out, imag_out]).astype(jnp.bfloat16)

def reference(snapshots, basis, mass_table, elem_kind, offsets):
    dft_table = spectral_table(offsets, NT, F, RECORD)
    table_flat = dft_table.reshape(2 * F * NB, RECORD)
    entries = NVAR * NPTS
    block_pts = math.gcd(NPTS, 4096)
    block_count = NPTS // block_pts
    block_elems = block_pts // ELEM_PTS
    block_ids = jnp.arange(block_count, dtype=jnp.int32)

    def block_data(block_index):
        first_pt = (block_index * block_pts).astype(jnp.int32)
        record_blk = lax.dynamic_slice_in_dim(snapshots, first_pt, block_pts, 2)
        kinds_blk = lax.dynamic_slice_in_dim(elem_kind, (block_index * block_elems).astype(jnp.int32), block_elems, 0)
        mass_blk = mass_table[kinds_blk]
        return (record_blk.reshape(RECORD, NVAR * block_pts), mass_blk, first_pt)

    def coefficient_part(block_index):
        record_flat, mass_blk, first_pt = block_data(block_index)
        basis_blk = lax.dynamic_slice_in_dim(basis, first_pt, block_pts, 4)
        spectra = jnp.dot(table_flat, record_flat, preferred_element_type=jnp.float32)
        weighted = apply_mass(spectra.reshape(2, F, NB, NVAR, block_pts), mass_blk).astype(jnp.bfloat16)
        weighted = weighted.reshape(2, F, NB, NVAR * block_pts).astype(jnp.float32)
        mode_rows = basis_blk.reshape(2, F, RANK, NVAR * block_pts).astype(jnp.float32)
        return project(mode_rows, weighted)
    coeffs = lax.optimization_barrier(jnp.sum(lax.map(coefficient_part, block_ids), axis=0)) / math.sqrt(entries)
    kernel = time_kernel(dft_table, coeffs).reshape(2 * F * RANK, RECORD)

    def field_block(block_index):
        record_flat, mass_blk, first_pt = block_data(block_index)
        fields = jnp.dot(kernel, record_flat, preferred_element_type=jnp.float32)
        return (fields.reshape(2, F, RANK, NVAR, block_pts), mass_blk)

    def energy_part(block_index):
        fields, mass_blk = field_block(block_index)
        massed = apply_mass(fields, mass_blk)
        return lax.optimization_barrier(jnp.sum(fields * massed, axis=(0, 3, 4)))
    energy = lax.optimization_barrier(jnp.sum(lax.map(energy_part, block_ids), axis=0))
    factor = 1.0 / jnp.sqrt(energy / entries + 1e-06)

    def output_part(block_index):
        fields, mass_blk = field_block(block_index)
        return (fields * factor[None, :, :, None, None]).astype(jnp.bfloat16)
    pieces = lax.map(output_part, block_ids)
    new_basis = jnp.moveaxis(pieces, 0, 4).reshape(2, F, RANK, NVAR, NPTS)
    return (coeffs, new_basis)
```

```python
import functools
import math

import jax
import jax.numpy as jnp
from jax import lax
from jax.experimental import pallas as pl
from jax.experimental.pallas import tpu as pltpu
from jax.sharding import PartitionSpec as P

NT = 256
GROUP = 8
LEVELS = 4
MESH = pl.DeviceIdType.MESH
BF = jnp.bfloat16
F32 = jnp.float32


def mm(a, b, contract):
    return lax.dot_general(a, b, (contract, ((), ())), preferred_element_type=F32)


def kernel(
    n_tm, n_sp, low, entries, chunks,
    snap, basis, mass_in, kinds_in, offs_in,
    sh, y_out,
    table, ub, xb, line, plane, yb, mass, kinds, offs, *rest,
):
    recs, (a_send, a_recv, l_sem, known, s1, r1, s2, r2, s3, r3) = rest[: len(chunks)], rest[len(chunks) :]
    tm = lax.axis_index("tm")
    sp = lax.axis_index("space")
    high = n_tm // low
    quart = n_tm // LEVELS
    lev, place = lax.div(tm, quart), lax.rem(tm, quart)
    edge = (lev == 0) | (lev == LEVELS - 1)
    inward = jnp.where(lev < LEVELS // 2, 1, -1)
    side = low * n_sp
    mid = n_tm // 2
    turn = lax.rem(tm + n_tm - n_tm // 4, n_tm)
    spot = lax.div(turn, mid) * (side // 2) + sp * mid + lax.rem(turn, mid)
    level = lax.div(tm, low)
    freqs = basis.shape[1]
    rows, pts = recs[0].shape[2:]
    groups = sh.shape[0] // (2 * GROUP * 8)
    record = n_tm * rows
    blocks = offs.shape[0]
    modes = basis.shape[3]
    upo = plane.shape[1]
    owners = xb.shape[0] // upo
    half = GROUP * blocks
    lanes = GROUP * modes

    def beside(p):
        r = lax.rem(p, side // 2)
        back = lax.div(p, side // 2) * mid + lax.rem(r, mid)
        return {"tm": lax.rem(back + n_tm // 4, n_tm), "space": lax.div(r, mid)}

    barrier = pltpu.get_barrier_semaphore()

    def signal(sem, to_tm, to_sp):
        pl.semaphore_signal(
            sem, inc=1, device_id={"tm": to_tm, "space": to_sp}, device_id_type=MESH
        )

    for dl in (1, -1, 0):

        def greet(i, carry):
            to = (lev + dl) * quart + lax.rem(place + i, quart)
            signal(barrier, to, sp)
            return carry

        @pl.when((lev + dl >= 0) & (lev + dl < LEVELS))
        def _():
            lax.fori_loop(1 if dl == 0 else 0, quart, greet, 0, unroll=side <= 32)

    def greet_side(i, carry):
        signal(barrier, tm, lax.rem(sp + i, n_sp))
        return carry

    lax.fori_loop(1, n_sp, greet_side, 0, unroll=side <= 32)
    loads = [
        pltpu.make_async_copy(offs_in, offs, l_sem.at[0]),
        pltpu.make_async_copy(kinds_in, kinds, l_sem.at[1]),
        pltpu.make_async_copy(mass_in, mass, l_sem.at[2]),
        pltpu.make_async_copy(basis, ub.at[:, pl.ds(0, freqs)], l_sem.at[3]),
    ]
    for cp in loads:
        cp.start()
    near = jnp.where(edge, 2, 3)
    pl.semaphore_wait(barrier, near * quart - 1 + n_sp - 1)

    def relay(stage):
        for dl in (1, -1):
            seen = lev - dl * (stage - 1)

            @pl.when((seen >= 0) & (seen < LEVELS) & (lev + dl >= 0) & (lev + dl < LEVELS))
            def _():
                signal(known.at[stage - 2], tm + dl * quart, sp)

    def learn(stage):
        for dl in (1, -1):

            @pl.when((lev + dl * stage >= 0) & (lev + dl * stage < LEVELS))
            def _():
                pl.semaphore_wait(known.at[stage - 2], 1)

    def send_level(ci, to_lev, first=0):
        v0, v1 = chunks[ci]

        def send(i, carry):
            to = to_lev * quart + lax.rem(place + i, quart)
            pltpu.make_async_remote_copy(
                snap.at[pl.ds(v0, v1 - v0), :, pl.ds(pl.multiple_of(to * pts, pts), pts)],
                recs[ci].at[tm], a_send.at[ci], a_recv.at[ci],
                device_id={"tm": to, "space": sp}, device_id_type=MESH,
            ).start()
            return carry

        lax.fori_loop(first, quart, send, 0, unroll=side <= 32)

    relay(2)
    for ci, (v0, v1) in enumerate(chunks):
        mine = snap.at[pl.ds(v0, v1 - v0), :, pl.ds(pl.multiple_of(tm * pts, pts), pts)]
        if ci == 0:
            send_level(ci, lev + inward)
            pl.when(jnp.logical_not(edge))(lambda: send_level(ci, lev - inward))
            send_level(ci, lev, 1)
            learn(2)
            relay(3)
            send_level(ci, lev + 2 * inward)
            learn(3)
            pl.when(edge)(lambda: send_level(ci, lev + 3 * inward))

            def tell(i, carry):
                signal(known.at[2], tm, lax.rem(sp + i, n_sp))
                return carry

            lax.fori_loop(1, n_sp, tell, 0, unroll=side <= 32)
        else:
            pl.when(edge)(lambda: send_level(ci, lev + 3 * inward))
            send_level(ci, lev + 2 * inward)
            send_level(ci, lev + inward)
            pl.when(jnp.logical_not(edge))(lambda: send_level(ci, lev - inward))
            send_level(ci, lev, 1)
        pltpu.make_async_copy(mine, recs[ci].at[tm], a_recv.at[ci]).start()

    loads[0].wait()
    row = lax.broadcasted_iota(jnp.int32, (blocks, record), 0)
    lag = lax.broadcasted_iota(jnp.int32, (blocks, record), 1)
    for b in range(blocks):
        lag = jnp.where(row == b, lag - offs[b], lag)
    inside = (lag >= 0) & (lag < NT)
    theta = jnp.clip(lag, 0, NT - 1).astype(F32) * (2.0 * math.pi / NT)
    c1, s1v = jnp.cos(theta), jnp.sin(theta)
    win = jnp.where(inside, (0.5 - 0.5 * c1) * (1.0 / math.sqrt(0.375 * NT)), 0.0)
    cc, ss = win, jnp.zeros_like(win)
    for f in range(0, groups * GROUP, 2):
        c_next, s_next = cc * c1 - ss * s1v, ss * c1 + cc * s1v
        at = (f // GROUP) * 2 * half + (f % GROUP) * blocks
        table[at : at + 2 * blocks] = jnp.concatenate([cc, c_next], axis=0).astype(BF)
        table[at + half : at + half + 2 * blocks] = jnp.concatenate([-ss, -s_next], axis=0).astype(BF)
        cc, ss = c_next * c1 - s_next * s1v, s_next * c1 + c_next * s1v

    loads[1].wait()
    loads[2].wait()
    size = mass.shape[1]
    elems = pts // size
    strips = []
    for e in range(elems):
        kind = jnp.full((size, size), kinds[e], jnp.int32)
        blk = mass[0]
        for k in range(1, mass.shape[0]):
            blk = jnp.where(kind == k, mass[k], blk)
        zero = jnp.zeros_like(blk)
        strips.append(jnp.concatenate([blk if j == e else zero for j in range(elems)], axis=1))
    m_all = jnp.concatenate(strips, axis=0)
    m_hi = m_all.astype(BF)
    m_lo = (m_all - m_hi.astype(F32)).astype(BF)
    m_stack = jnp.concatenate([m_hi, m_hi, m_lo], axis=0)

    loads[3].wait()
    ub[:, freqs:] = jnp.zeros((2, groups * GROUP - freqs) + ub.shape[2:], BF)

    row_f = lax.broadcasted_iota(jnp.int32, (GROUP, blocks, lanes), 0)
    lane = lax.broadcasted_iota(jnp.int32, (GROUP, blocks, lanes), 2)
    diag_k = row_f == lane // modes
    diag_b = row_f == (lane % half) // blocks
    lane2 = lax.broadcasted_iota(jnp.int32, (blocks, lanes), 1)

    def fold(full, mask):
        return jnp.sum(jnp.where(mask, full.reshape(GROUP, blocks, lanes), 0.0), axis=0)

    total = [None] * (3 * groups)
    for ci, (v0, v1) in enumerate(chunks):
        rec = recs[ci]
        pltpu.make_async_copy(rec, rec, a_recv.at[ci]).wait()
        count = v1 - v0
        x = jnp.concatenate([rec[:, v].reshape(record, pts) for v in range(count)], axis=1)
        spec = mm(table[...], x, ((1,), (0,)))
        s_hi = spec.astype(BF)
        s_lo = (spec - s_hi.astype(F32)).astype(BF)
        sh[:, v0 * pts : v1 * pts] = s_hi
        wts = []
        for v in range(count):
            cut = slice(v * pts, (v + 1) * pts)
            lhs = jnp.concatenate([s_hi[:, cut], s_lo[:, cut], s_hi[:, cut]], axis=1)
            wts.append(mm(lhs, m_stack, ((1,), (0,))).astype(BF))
        wt = jnp.concatenate(wts, axis=1)
        for g in range(groups):
            top = g * 2 * half
            f0 = g * GROUP
            u = [
                jnp.concatenate(
                    [ub[c, f0 : f0 + GROUP, v].reshape(lanes, pts) for v in range(v0, v1)], axis=1
                )
                for c in range(2)
            ]
            lhs = jnp.concatenate(u + [s_hi[top : top + 2 * half]], axis=0)
            full = mm(wt[top : top + 2 * half], lhs, ((1,), (1,)))
            rr = fold(full[:half, :lanes], diag_k)
            ri = fold(full[:half, lanes : 2 * lanes], diag_k)
            ir = fold(full[half:, :lanes], diag_k)
            ii = fold(full[half:, lanes : 2 * lanes], diag_k)
            p_r = fold(full[:half, 2 * lanes :], diag_b)
            p_i = pltpu.roll(fold(full[half:, 2 * lanes :], diag_b), half, 1)
            new = [rr + ii, ir - ri, jnp.where(lane2 < half, p_r + p_i, p_i - p_r)]
            for j in range(3):
                at = 3 * g + j
                total[at] = new[j] if ci == 0 else total[at] + new[j]
    for at in range(3 * groups):
        xb[at] = total[at]

    mine = pl.ds(spot * upo, upo)
    pl.semaphore_wait(known.at[2], n_sp - 1)

    def scatter(i, carry):
        o = lax.rem(spot + i, owners)

        @pl.when(o != spot)
        def _():
            pltpu.make_async_remote_copy(
                xb.at[pl.ds(o * upo, upo)], plane.at[spot], s1, r1,
                device_id=beside(o), device_id_type=MESH,
            ).start()

        return carry

    lax.fori_loop(0, owners, scatter, 0, unroll=side <= 32)

    def wait_bytes(ref, sem):
        pltpu.make_async_copy(ref, ref, sem).wait()

    @pl.when(spot < owners)
    def _():
        plane[spot] = xb[mine]
        wait_bytes(plane.at[pl.ds(0, side - 1)], r1)
        line[level] = jnp.sum(plane[...], axis=0)

        def exchange(i, carry):
            to = lax.rem(level + i, high) * low + lax.rem(tm, low)
            pltpu.make_async_remote_copy(
                line.at[level], line.at[level], s2, r2,
                device_id={"tm": to, "space": sp}, device_id_type=MESH,
            ).start()
            return carry

        if high > 1:
            lax.fori_loop(1, high, exchange, 0)
            wait_bytes(line.at[pl.ds(0, high - 1)], r2)
        yb[mine] = jnp.sum(line[...], axis=0)

        def gather(i, carry):
            pltpu.make_async_remote_copy(
                yb.at[mine], yb.at[mine], s3, r3,
                device_id=beside(lax.rem(spot + i, side)), device_id_type=MESH,
            ).start()
            return carry

        lax.fori_loop(1, side, gather, 0, unroll=side <= 32)
        wait_bytes(yb.at[pl.ds(0, (owners - 1) * upo)], r3)

    @pl.when(spot >= owners)
    def _():
        wait_bytes(yb, r3)

    y_out[...] = yb[...]
    for ci in range(len(chunks)):
        wait_bytes(recs[ci].at[pl.ds(0, n_tm - 1)], a_send.at[ci])

    @pl.when(spot < owners)
    def _():
        wait_bytes(xb.at[pl.ds(0, (owners - 1) * upo)], s1)
        if high > 1:
            wait_bytes(line.at[pl.ds(0, high - 1)], s2)
        wait_bytes(plane.at[pl.ds(0, side - 1)], s3)

    @pl.when(spot >= owners)
    def _():
        wait_bytes(xb, s1)


def finish(entries, yb, sh, coef_out, new_out, ob, o_sem):
    freqs, nvar, modes, pts = new_out.shape[1:]
    blocks = coef_out.shape[1]
    half = GROUP * blocks
    lanes = GROUP * modes
    groups = -(-freqs // GROUP)
    row_f = lax.broadcasted_iota(jnp.int32, (GROUP, blocks, lanes), 0)
    lane = lax.broadcasted_iota(jnp.int32, (GROUP, blocks, lanes), 2)
    diag_k = row_f == lane // modes
    diag_b = row_f == (lane % half) // blocks
    lane2 = lax.broadcasted_iota(jnp.int32, (blocks, lanes), 1)
    scale = 1.0 / math.sqrt(entries)

    def spread_rows(val, mask):
        big = jnp.broadcast_to(val[None], (GROUP, blocks, lanes))
        return jnp.where(mask, big, 0.0).reshape(half, lanes)

    copies, held = [], []
    for g in range(groups):
        top = g * 2 * half
        f0 = g * GROUP
        nf = min(GROUP, freqs - f0)
        co = [yb[3 * g + c] * scale for c in range(2)]
        held.append(co)
        cr, ci = [v.astype(BF).astype(F32) for v in co]
        gram = yb[3 * g + 2]
        d_r, d_i = spread_rows(cr, diag_k), spread_rows(ci, diag_k)
        turned = pltpu.roll(gram, half, 1)
        turned = jnp.where(lane2 < half, -turned, turned)
        quad = jnp.concatenate([spread_rows(gram, diag_b), spread_rows(turned, diag_b)], axis=0)
        vec = jnp.concatenate([d_r, d_i], axis=0)
        energy = jnp.sum(vec * mm(quad.astype(BF), vec.astype(BF), ((1,), (0,))), axis=0, keepdims=True)
        factor = 1.0 / jnp.sqrt(energy / entries + 1e-06)
        fac = jnp.transpose(jnp.broadcast_to(factor, (pts, lanes)))
        s_g = sh[top : top + 2 * half]
        for c in range(2):
            d = jnp.concatenate([d_r, -d_i] if c == 0 else [d_i, d_r], axis=0)
            field = mm(jnp.transpose(d).astype(BF), s_g, ((1,), (0,)))
            for v in range(nvar):
                val = (field[:, v * pts : (v + 1) * pts] * fac).astype(BF).reshape(GROUP, modes, pts)
                ob[c, f0 : f0 + nf, v] = val[:nf]
        cp = pltpu.make_async_copy(ob.at[:, pl.ds(f0, nf)], new_out.at[:, pl.ds(f0, nf)], o_sem.at[g])
        cp.start()
        copies.append(cp)

    mode_row = lax.broadcasted_iota(jnp.int32, (blocks, modes, lanes), 1)
    pick = mode_row == lax.broadcasted_iota(jnp.int32, (blocks, modes, lanes), 2) % modes
    e_row = lax.broadcasted_iota(jnp.int32, (lanes, freqs), 0) // modes
    e_col = lax.broadcasted_iota(jnp.int32, (lanes, freqs), 1)
    moves = [jnp.where(e_col == e_row + g * GROUP, 1.0, 0.0).astype(BF) for g in range(groups)]
    move = jnp.concatenate(moves + moves, axis=0)
    for c in range(2):
        his, los = [], []
        for g in range(groups):
            val = held[g][c]
            if g == groups - 1:
                val = jnp.where(lane2 < (freqs - g * GROUP) * modes, val, 0.0)
            hi = val.astype(BF).astype(F32)
            for part, to in ((hi, his), (val - hi, los)):
                big = jnp.broadcast_to(part[:, None, :], (blocks, modes, lanes))
                to.append(jnp.where(pick, big, 0.0).reshape(blocks * modes, lanes).astype(BF))
        moved = mm(jnp.concatenate(his + los, axis=1), move, ((1,), (0,)))
        coef_out[c] = moved.reshape(blocks, modes, freqs)
    for cp in copies:
        cp.wait()


def solution(mesh):
    n_tm, n_sp = mesh.shape["tm"], mesh.shape["space"]
    n = n_tm * n_sp

    def on_device(snapshots, basis, mass_table, elem_kind, offsets):
        rows, nvar, slab = snapshots.shape
        _, freqs, modes, _, pts = basis.shape
        blocks = offsets.shape[0]
        groups = -(-freqs // GROUP)
        entries = nvar * pts * n
        units = 3 * groups
        low = n_tm
        side = low * n_sp
        upo = -(-units // side)
        owners = -(-units // upo)
        table_rows = groups * 2 * GROUP * blocks
        unit = (blocks, GROUP * modes)
        chunks = tuple((v, min(v + 2, nvar)) for v in range(0, nvar, 2))
        snap = jnp.transpose(snapshots, (1, 0, 2))
        base = jnp.transpose(basis, (0, 1, 3, 2, 4))
        hbm = pl.BlockSpec(memory_space=pltpu.HBM)
        vmem = pl.BlockSpec(memory_space=pltpu.VMEM)
        spec, total = pl.pallas_call(
            functools.partial(kernel, n_tm, n_sp, low, entries, chunks),
            out_shape=(
                jax.ShapeDtypeStruct((table_rows, nvar * pts), BF),
                jax.ShapeDtypeStruct((owners * upo,) + unit, F32),
            ),
            in_specs=[hbm] * 5,
            out_specs=(vmem, vmem),
            scratch_shapes=[
                pltpu.VMEM((table_rows, rows * n_tm), BF),
                pltpu.VMEM((2, groups * GROUP, nvar, modes, pts), BF),
                pltpu.VMEM((owners * upo,) + unit, F32),
                pltpu.VMEM((n_tm // low, upo) + unit, F32),
                pltpu.VMEM((side, upo) + unit, F32),
                pltpu.VMEM((owners * upo,) + unit, F32),
                pltpu.VMEM(mass_table.shape, F32),
                pltpu.SMEM(elem_kind.shape, jnp.int32),
                pltpu.SMEM(offsets.shape, jnp.int32),
            ]
            + [pltpu.VMEM((n_tm, v1 - v0, rows, pts), BF) for v0, v1 in chunks]
            + [
                pltpu.SemaphoreType.DMA((len(chunks),)),
                pltpu.SemaphoreType.DMA((len(chunks),)),
                pltpu.SemaphoreType.DMA((4,)),
                pltpu.SemaphoreType.REGULAR((3,)),
            ]
            + [pltpu.SemaphoreType.DMA] * 6,
            compiler_params=pltpu.CompilerParams(
                collective_id=0, has_side_effects=True, vmem_limit_bytes=48 * 1024 * 1024
            ),
        )(*[pltpu.with_memory_space_constraint(a, pltpu.HBM) for a in (snap, base, mass_table, elem_kind, offsets)])
        coef, new = pl.pallas_call(
            functools.partial(finish, entries),
            out_shape=(
                jax.ShapeDtypeStruct((2, blocks, modes, freqs), F32),
                jax.ShapeDtypeStruct(base.shape, BF),
            ),
            in_specs=[vmem, vmem],
            out_specs=(vmem, hbm),
            scratch_shapes=[pltpu.VMEM(base.shape, BF), pltpu.SemaphoreType.DMA((groups,))],
            compiler_params=pltpu.CompilerParams(vmem_limit_bytes=32 * 1024 * 1024),
        )(total, spec)
        return jnp.transpose(coef, (0, 3, 1, 2)), jnp.transpose(new, (0, 1, 3, 2, 4))

    return jax.shard_map(
        on_device,
        mesh=mesh,
        in_specs=(
            P("tm", None, "space"),
            P(None, None, None, None, ("space", "tm")),
            P(),
            P(("space", "tm")),
            P(),
        ),
        out_specs=(P(), P(None, None, None, None, ("space", "tm"))),
        check_vma=False,
    )
```

```python
import functools
import math

import jax
import jax.numpy as jnp
from jax import lax
from jax.experimental import pallas as pl
from jax.experimental.pallas import tpu as pltpu
from jax.sharding import PartitionSpec as P

NT = 256
GROUP = 8
LEVELS = 4
MESH = pl.DeviceIdType.MESH
BF = jnp.bfloat16
F32 = jnp.float32


def owner_list(n_tm, n_sp, count):
    quart = n_tm // LEVELS
    first = [(quart, 0), (2 * quart, 0), (quart + 2, 0), (quart, 1)]
    spots = [(t + c, s) for t, s in first for c in range(2)]
    spots += [(t, s) for s in range(n_sp) for t in range(n_tm) if (t, s) not in spots]
    return tuple(p for p in spots if p[0] < n_tm and p[1] < n_sp)[:count]


def mm(a, b, contract):
    return lax.dot_general(a, b, (contract, ((), ())), preferred_element_type=F32)


def kernel(
    n_tm, n_sp, owners, entries, chunks,
    snap, basis, mass_in, kinds_in, offs_in,
    sh, y_out,
    table, ub, xb, plane, yb, mass, kinds, offs, *rest,
):
    recs, (a_send, a_recv, l_sem, known, s1, r1, s2, r2) = rest[: len(chunks)], rest[len(chunks) :]
    tm = lax.axis_index("tm")
    sp = lax.axis_index("space")
    side = n_tm * n_sp
    scale = 1.0 / math.sqrt(entries)
    here = sp * n_tm + tm
    is_own = [(tm == o_tm) & (sp == o_sp) for o_tm, o_sp in owners]
    owner = functools.reduce(jnp.logical_or, is_own)
    spot = sum(jnp.where(m, o, 0) for o, m in enumerate(is_own))
    quart = n_tm // LEVELS
    lev, place = lax.div(tm, quart), lax.rem(tm, quart)
    edge = (lev == 0) | (lev == LEVELS - 1)
    inward = jnp.where(lev < LEVELS // 2, 1, -1)
    freqs = basis.shape[1]
    rows, pts = recs[0].shape[2:]
    groups = sh.shape[0] // (2 * GROUP * 8)
    record = n_tm * rows
    blocks = offs.shape[0]
    modes = basis.shape[3]
    upo = plane.shape[1]
    half = GROUP * blocks
    lanes = GROUP * modes

    barrier = pltpu.get_barrier_semaphore()

    def signal(sem, to_tm, to_sp):
        pl.semaphore_signal(
            sem, inc=1, device_id={"tm": to_tm, "space": to_sp}, device_id_type=MESH
        )

    for dl in (1, -1, 0):

        def greet(i, carry):
            to = (lev + dl) * quart + lax.rem(place + i, quart)
            signal(barrier, to, sp)
            return carry

        @pl.when((lev + dl >= 0) & (lev + dl < LEVELS))
        def _():
            lax.fori_loop(1 if dl == 0 else 0, quart, greet, 0, unroll=side <= 32)

    def greet_side(i, carry):
        signal(barrier, tm, lax.rem(sp + i, n_sp))
        return carry

    lax.fori_loop(1, n_sp, greet_side, 0, unroll=side <= 32)
    loads = [
        pltpu.make_async_copy(offs_in, offs, l_sem.at[0]),
        pltpu.make_async_copy(kinds_in, kinds, l_sem.at[1]),
        pltpu.make_async_copy(mass_in, mass, l_sem.at[2]),
        pltpu.make_async_copy(basis, ub.at[:, pl.ds(0, freqs)], l_sem.at[3]),
    ]
    for cp in loads:
        cp.start()
    near = jnp.where(edge, 2, 3)
    pl.semaphore_wait(barrier, near * quart - 1 + n_sp - 1)

    def relay(stage):
        for dl in (1, -1):
            seen = lev - dl * (stage - 1)

            @pl.when((seen >= 0) & (seen < LEVELS) & (lev + dl >= 0) & (lev + dl < LEVELS))
            def _():
                signal(known.at[stage - 2], tm + dl * quart, sp)

    def learn(stage):
        for dl in (1, -1):

            @pl.when((lev + dl * stage >= 0) & (lev + dl * stage < LEVELS))
            def _():
                pl.semaphore_wait(known.at[stage - 2], 1)

    def send_level(ci, to_lev, first=0):
        v0, v1 = chunks[ci]

        def send(i, carry):
            to = to_lev * quart + lax.rem(place + i, quart)
            pltpu.make_async_remote_copy(
                snap.at[pl.ds(v0, v1 - v0), :, pl.ds(pl.multiple_of(to * pts, pts), pts)],
                recs[ci].at[tm], a_send.at[ci], a_recv.at[ci],
                device_id={"tm": to, "space": sp}, device_id_type=MESH,
            ).start()
            return carry

        lax.fori_loop(first, quart, send, 0, unroll=side <= 32)

    relay(2)
    for ci, (v0, v1) in enumerate(chunks):
        mine = snap.at[pl.ds(v0, v1 - v0), :, pl.ds(pl.multiple_of(tm * pts, pts), pts)]
        if ci == 0:
            send_level(ci, lev + inward)
            pl.when(jnp.logical_not(edge))(lambda: send_level(ci, lev - inward))
            send_level(ci, lev, 1)
            learn(2)
            relay(3)
            send_level(ci, lev + 2 * inward)
            learn(3)
            pl.when(edge)(lambda: send_level(ci, lev + 3 * inward))

            def tell(i, carry):
                signal(known.at[2], tm, lax.rem(sp + i, n_sp))
                return carry

            lax.fori_loop(1, n_sp, tell, 0, unroll=side <= 32)
        else:
            pl.when(edge)(lambda: send_level(ci, lev + 3 * inward))
            send_level(ci, lev + 2 * inward)
            send_level(ci, lev + inward)
            pl.when(jnp.logical_not(edge))(lambda: send_level(ci, lev - inward))
            send_level(ci, lev, 1)
        pltpu.make_async_copy(mine, recs[ci].at[tm], a_recv.at[ci]).start()

    loads[0].wait()
    row = lax.broadcasted_iota(jnp.int32, (blocks, record), 0)
    lag = lax.broadcasted_iota(jnp.int32, (blocks, record), 1)
    for b in range(blocks):
        lag = jnp.where(row == b, lag - offs[b], lag)
    inside = (lag >= 0) & (lag < NT)
    theta = jnp.clip(lag, 0, NT - 1).astype(F32) * (2.0 * math.pi / NT)
    c1, s1v = jnp.cos(theta), jnp.sin(theta)
    win = jnp.where(inside, (0.5 - 0.5 * c1) * (1.0 / math.sqrt(0.375 * NT)), 0.0)
    cc, ss = win, jnp.zeros_like(win)
    for f in range(0, groups * GROUP, 2):
        c_next, s_next = cc * c1 - ss * s1v, ss * c1 + cc * s1v
        at = (f // GROUP) * 2 * half + (f % GROUP) * blocks
        table[at : at + 2 * blocks] = jnp.concatenate([cc, c_next], axis=0).astype(BF)
        table[at + half : at + half + 2 * blocks] = jnp.concatenate([-ss, -s_next], axis=0).astype(BF)
        cc, ss = c_next * c1 - s_next * s1v, s_next * c1 + c_next * s1v

    loads[1].wait()
    loads[2].wait()
    size = mass.shape[1]
    elems = pts // size
    strips = []
    for e in range(elems):
        kind = jnp.full((size, size), kinds[e], jnp.int32)
        blk = mass[0]
        for k in range(1, mass.shape[0]):
            blk = jnp.where(kind == k, mass[k], blk)
        zero = jnp.zeros_like(blk)
        strips.append(jnp.concatenate([blk if j == e else zero for j in range(elems)], axis=1))
    m_all = jnp.concatenate(strips, axis=0)
    m_hi = m_all.astype(BF)
    m_lo = (m_all - m_hi.astype(F32)).astype(BF)
    m_stack = jnp.concatenate([m_hi, m_hi, m_lo], axis=0)

    loads[3].wait()
    ub[:, freqs:] = jnp.zeros((2, groups * GROUP - freqs) + ub.shape[2:], BF)

    row_f = lax.broadcasted_iota(jnp.int32, (GROUP, blocks, lanes), 0)
    lane = lax.broadcasted_iota(jnp.int32, (GROUP, blocks, lanes), 2)
    diag_k = row_f == lane // modes
    diag_b = row_f == (lane % half) // blocks
    lane2 = lax.broadcasted_iota(jnp.int32, (blocks, lanes), 1)

    def fold(full, mask):
        return jnp.sum(jnp.where(mask, full.reshape(GROUP, blocks, lanes), 0.0), axis=0)

    total = [None] * (3 * groups)
    for ci, (v0, v1) in enumerate(chunks):
        rec = recs[ci]
        pltpu.make_async_copy(rec, rec, a_recv.at[ci]).wait()
        count = v1 - v0
        x = jnp.concatenate([rec[:, v].reshape(record, pts) for v in range(count)], axis=1)
        spec = mm(table[...], x, ((1,), (0,)))
        s_hi = spec.astype(BF)
        s_lo = (spec - s_hi.astype(F32)).astype(BF)
        sh[:, v0 * pts : v1 * pts] = s_hi
        wts = []
        for v in range(count):
            cut = slice(v * pts, (v + 1) * pts)
            lhs = jnp.concatenate([s_hi[:, cut], s_lo[:, cut], s_hi[:, cut]], axis=1)
            wts.append(mm(lhs, m_stack, ((1,), (0,))).astype(BF))
        wt = jnp.concatenate(wts, axis=1)
        for g in range(groups):
            top = g * 2 * half
            f0 = g * GROUP
            u = [
                jnp.concatenate(
                    [ub[c, f0 : f0 + GROUP, v].reshape(lanes, pts) for v in range(v0, v1)], axis=1
                )
                for c in range(2)
            ]
            lhs = jnp.concatenate(u + [s_hi[top : top + 2 * half]], axis=0)
            full = mm(wt[top : top + 2 * half], lhs, ((1,), (1,)))
            rr = fold(full[:half, :lanes], diag_k)
            ri = fold(full[:half, lanes : 2 * lanes], diag_k)
            ir = fold(full[half:, :lanes], diag_k)
            ii = fold(full[half:, lanes : 2 * lanes], diag_k)
            p_r = fold(full[:half, 2 * lanes :], diag_b)
            p_i = pltpu.roll(fold(full[half:, 2 * lanes :], diag_b), half, 1)
            new = [(rr + ii) * scale, (ir - ri) * scale, jnp.where(lane2 < half, p_r + p_i, p_i - p_r)]
            for j in range(3):
                at = 3 * g + j
                total[at] = new[j] if ci == 0 else total[at] + new[j]
    empty = jnp.zeros((blocks, lanes), F32)
    total += [empty] * (2 * xb.shape[0] - len(total))
    for at in range(xb.shape[0]):
        xb[at] = jnp.concatenate(total[2 * at : 2 * at + 2], axis=0).astype(BF)

    pl.semaphore_wait(known.at[2], n_sp - 1)
    for o, (o_tm, o_sp) in enumerate(owners):

        @pl.when((tm != o_tm) | (sp != o_sp))
        def _():
            pltpu.make_async_remote_copy(
                xb.at[pl.ds(o * upo, upo)], plane.at[here], s1, r1,
                device_id={"tm": o_tm, "space": o_sp}, device_id_type=MESH,
            ).start()

    def wait_bytes(ref, sem):
        pltpu.make_async_copy(ref, ref, sem).wait()

    @pl.when(owner)
    def _():
        mine = pl.ds(spot * upo, upo)
        plane[here] = xb[mine]
        wait_bytes(plane.at[pl.ds(0, side - 1)], r1)
        yb[mine] = jnp.sum(plane[...].astype(F32), axis=0).astype(BF)

        def gather(i, carry):
            @pl.when(i != tm * n_sp + sp)
            def _():
                pltpu.make_async_remote_copy(
                    yb.at[mine], yb.at[mine], s2, r2,
                    device_id={"tm": lax.div(i, n_sp), "space": lax.rem(i, n_sp)}, device_id_type=MESH,
                ).start()

            return carry

        lax.fori_loop(0, side, gather, 0, unroll=side <= 32)
        wait_bytes(yb.at[pl.ds(0, (len(owners) - 1) * upo)], r2)

    @pl.when(jnp.logical_not(owner))
    def _():
        wait_bytes(yb, r2)

    y_out[...] = yb[...]
    for ci in range(len(chunks)):
        wait_bytes(recs[ci].at[pl.ds(0, n_tm - 1)], a_send.at[ci])

    @pl.when(owner)
    def _():
        wait_bytes(xb.at[pl.ds(0, (len(owners) - 1) * upo)], s1)
        wait_bytes(plane.at[pl.ds(0, side - 1)], s2)

    @pl.when(jnp.logical_not(owner))
    def _():
        wait_bytes(xb, s1)


def finish(entries, yb, sh, coef_out, new_out, ob, o_sem):
    freqs, nvar, modes, pts = new_out.shape[1:]
    blocks = coef_out.shape[1]
    half = GROUP * blocks
    lanes = GROUP * modes
    groups = -(-freqs // GROUP)
    row_f = lax.broadcasted_iota(jnp.int32, (GROUP, blocks, lanes), 0)
    lane = lax.broadcasted_iota(jnp.int32, (GROUP, blocks, lanes), 2)
    diag_k = row_f == lane // modes
    diag_b = row_f == (lane % half) // blocks
    lane2 = lax.broadcasted_iota(jnp.int32, (blocks, lanes), 1)

    def unit(at):
        return pairs[at // 2][at % 2 * blocks : (at % 2 + 1) * blocks]

    pairs = [yb[at].astype(F32) for at in range(yb.shape[0])]

    def spread_rows(val, mask):
        big = jnp.broadcast_to(val[None], (GROUP, blocks, lanes))
        return jnp.where(mask, big, 0.0).reshape(half, lanes)

    copies, held = [], []
    for g in range(groups):
        top = g * 2 * half
        f0 = g * GROUP
        nf = min(GROUP, freqs - f0)
        cr, ci = unit(3 * g), unit(3 * g + 1)
        held.append((cr, ci))
        gram = unit(3 * g + 2)
        d_r, d_i = spread_rows(cr, diag_k), spread_rows(ci, diag_k)
        turned = pltpu.roll(gram, half, 1)
        turned = jnp.where(lane2 < half, -turned, turned)
        quad = jnp.concatenate([spread_rows(gram, diag_b), spread_rows(turned, diag_b)], axis=0)
        vec = jnp.concatenate([d_r, d_i], axis=0)
        energy = jnp.sum(vec * mm(quad.astype(BF), vec.astype(BF), ((1,), (0,))), axis=0, keepdims=True)
        factor = 1.0 / jnp.sqrt(energy / entries + 1e-06)
        fac = jnp.transpose(jnp.broadcast_to(factor, (pts, lanes)))
        s_g = sh[top : top + 2 * half]
        for c in range(2):
            d = jnp.concatenate([d_r, -d_i] if c == 0 else [d_i, d_r], axis=0)
            field = mm(jnp.transpose(d).astype(BF), s_g, ((1,), (0,)))
            for v in range(nvar):
                val = (field[:, v * pts : (v + 1) * pts] * fac).astype(BF).reshape(GROUP, modes, pts)
                ob[c, f0 : f0 + nf, v] = val[:nf]
        cp = pltpu.make_async_copy(ob.at[:, pl.ds(f0, nf)], new_out.at[:, pl.ds(f0, nf)], o_sem.at[g])
        cp.start()
        copies.append(cp)

    mode_row = lax.broadcasted_iota(jnp.int32, (blocks, modes, lanes), 1)
    pick = mode_row == lax.broadcasted_iota(jnp.int32, (blocks, modes, lanes), 2) % modes
    e_row = lax.broadcasted_iota(jnp.int32, (lanes, freqs), 0) // modes
    e_col = lax.broadcasted_iota(jnp.int32, (lanes, freqs), 1)
    moves = [jnp.where(e_col == e_row + g * GROUP, 1.0, 0.0).astype(BF) for g in range(groups)]
    move = jnp.concatenate(moves, axis=0)
    for c in range(2):
        rows = []
        for g in range(groups):
            val = held[g][c]
            if g == groups - 1:
                val = jnp.where(lane2 < (freqs - g * GROUP) * modes, val, 0.0)
            big = jnp.broadcast_to(val[:, None, :], (blocks, modes, lanes))
            rows.append(jnp.where(pick, big, 0.0).reshape(blocks * modes, lanes).astype(BF))
        moved = mm(jnp.concatenate(rows, axis=1), move, ((1,), (0,)))
        coef_out[c] = moved.reshape(blocks, modes, freqs)
    for cp in copies:
        cp.wait()


def solution(mesh):
    n_tm, n_sp = mesh.shape["tm"], mesh.shape["space"]
    n = n_tm * n_sp

    def on_device(snapshots, basis, mass_table, elem_kind, offsets):
        rows, nvar, slab = snapshots.shape
        _, freqs, modes, _, pts = basis.shape
        blocks = offsets.shape[0]
        groups = -(-freqs // GROUP)
        entries = nvar * pts * n
        pairs = -(-3 * groups // 2)
        side = n_tm * n_sp
        upo = -(-pairs // side)
        owners = owner_list(n_tm, n_sp, -(-pairs // upo))
        table_rows = groups * 2 * GROUP * blocks
        unit = (2 * blocks, GROUP * modes)
        chunks = tuple((v, min(v + 2, nvar)) for v in range(0, nvar, 2))
        snap = jnp.transpose(snapshots, (1, 0, 2))
        base = jnp.transpose(basis, (0, 1, 3, 2, 4))
        hbm = pl.BlockSpec(memory_space=pltpu.HBM)
        vmem = pl.BlockSpec(memory_space=pltpu.VMEM)
        spec, total = pl.pallas_call(
            functools.partial(kernel, n_tm, n_sp, owners, entries, chunks),
            out_shape=(
                jax.ShapeDtypeStruct((table_rows, nvar * pts), BF),
                jax.ShapeDtypeStruct((len(owners) * upo,) + unit, BF),
            ),
            in_specs=[hbm] * 5,
            out_specs=(vmem, vmem),
            scratch_shapes=[
                pltpu.VMEM((table_rows, rows * n_tm), BF),
                pltpu.VMEM((2, groups * GROUP, nvar, modes, pts), BF),
                pltpu.VMEM((len(owners) * upo,) + unit, BF),
                pltpu.VMEM((side, upo) + unit, BF),
                pltpu.VMEM((len(owners) * upo,) + unit, BF),
                pltpu.VMEM(mass_table.shape, F32),
                pltpu.SMEM(elem_kind.shape, jnp.int32),
                pltpu.SMEM(offsets.shape, jnp.int32),
            ]
            + [pltpu.VMEM((n_tm, v1 - v0, rows, pts), BF) for v0, v1 in chunks]
            + [
                pltpu.SemaphoreType.DMA((len(chunks),)),
                pltpu.SemaphoreType.DMA((len(chunks),)),
                pltpu.SemaphoreType.DMA((4,)),
                pltpu.SemaphoreType.REGULAR((3,)),
            ]
            + [pltpu.SemaphoreType.DMA] * 4,
            compiler_params=pltpu.CompilerParams(
                collective_id=0, has_side_effects=True, vmem_limit_bytes=48 * 1024 * 1024
            ),
        )(*[pltpu.with_memory_space_constraint(a, pltpu.HBM) for a in (snap, base, mass_table, elem_kind, offsets)])
        coef, new = pl.pallas_call(
            functools.partial(finish, entries),
            out_shape=(
                jax.ShapeDtypeStruct((2, blocks, modes, freqs), F32),
                jax.ShapeDtypeStruct(base.shape, BF),
            ),
            in_specs=[vmem, vmem],
            out_specs=(vmem, hbm),
            scratch_shapes=[pltpu.VMEM(base.shape, BF), pltpu.SemaphoreType.DMA((groups,))],
            compiler_params=pltpu.CompilerParams(vmem_limit_bytes=32 * 1024 * 1024),
        )(total, spec)
        return jnp.transpose(coef, (0, 3, 1, 2)), jnp.transpose(new, (0, 1, 3, 2, 4))

    return jax.shard_map(
        on_device,
        mesh=mesh,
        in_specs=(
            P("tm", None, "space"),
            P(None, None, None, None, ("space", "tm")),
            P(),
            P(("space", "tm")),
            P(),
        ),
        out_specs=(P(), P(None, None, None, None, ("space", "tm"))),
        check_vma=False,
    )
```

```python
import functools
import math

import jax
import jax.numpy as jnp
from jax import lax
from jax.experimental import pallas as pl
from jax.experimental.pallas import tpu as pltpu
from jax.sharding import PartitionSpec as P

NT = 256
GROUP = 8
LEVELS = 4
MESH = pl.DeviceIdType.MESH
BF = jnp.bfloat16
F32 = jnp.float32


def owner_list(n_tm, n_sp, count):
    quart = n_tm // LEVELS
    first = [(quart, 0), (2 * quart, 0), (quart + 2, 0), (quart, 1)]
    spots = [(t + c, s) for t, s in first for c in range(2)]
    spots += [(t, s) for s in range(n_sp) for t in range(n_tm) if (t, s) not in spots]
    return tuple(p for p in spots if p[0] < n_tm and p[1] < n_sp)[:count]


def mm(a, b, contract):
    return lax.dot_general(a, b, (contract, ((), ())), preferred_element_type=F32)


def swap_halves(x, half):
    lanes = x.shape[1]
    if 2 * half == lanes:
        return pltpu.roll(x, half, 1)
    lane = lax.broadcasted_iota(jnp.int32, x.shape, 1)
    return jnp.where(lane < half, pltpu.roll(x, lanes - half, 1), pltpu.roll(x, half, 1))


def freq_mask(nf, rows, lanes, blocks):
    row_f = lax.broadcasted_iota(jnp.int32, (nf, rows, lanes), 0)
    lane = lax.broadcasted_iota(jnp.int32, (nf, rows, lanes), 2)
    half = nf * blocks
    return (row_f == lane % half // blocks) & (lane < 2 * half)


def kernel(
    n_tm, n_sp, owners, entries, chunks,
    snap, basis, mass_in, kinds_in, offs_in,
    sh, y_out,
    table, ub, xb, plane, yb, mass, kinds, offs, *rest,
):
    recs, (a_send, a_recv, l_sem, known, s1, r1, s2, r2) = rest[: len(chunks)], rest[len(chunks) :]
    tm = lax.axis_index("tm")
    sp = lax.axis_index("space")
    side = n_tm * n_sp
    scale = 1.0 / math.sqrt(entries)
    here = sp * n_tm + tm
    is_own = [(tm == o_tm) & (sp == o_sp) for o_tm, o_sp in owners]
    owner = functools.reduce(jnp.logical_or, is_own)
    spot = sum(jnp.where(m, o, 0) for o, m in enumerate(is_own))
    quart = n_tm // LEVELS
    lev, place = lax.div(tm, quart), lax.rem(tm, quart)
    edge = (lev == 0) | (lev == LEVELS - 1)
    inward = jnp.where(lev < LEVELS // 2, 1, -1)
    freqs = basis.shape[1]
    rows, pts = recs[0].shape[2:]
    groups = -(-freqs // GROUP)
    counts = [min(GROUP, freqs - g * GROUP) for g in range(groups)]
    record = n_tm * rows
    blocks = offs.shape[0]
    modes = basis.shape[3]
    upo = plane.shape[1]
    lanes = 2 * GROUP * blocks

    barrier = pltpu.get_barrier_semaphore()

    def signal(sem, to_tm, to_sp):
        pl.semaphore_signal(
            sem, inc=1, device_id={"tm": to_tm, "space": to_sp}, device_id_type=MESH
        )

    for dl in (1, -1, 0):

        def greet(i, carry):
            to = (lev + dl) * quart + lax.rem(place + i, quart)
            signal(barrier, to, sp)
            return carry

        @pl.when((lev + dl >= 0) & (lev + dl < LEVELS))
        def _():
            lax.fori_loop(1 if dl == 0 else 0, quart, greet, 0, unroll=side <= 32)

    def greet_side(i, carry):
        signal(barrier, tm, lax.rem(sp + i, n_sp))
        return carry

    lax.fori_loop(1, n_sp, greet_side, 0, unroll=side <= 32)
    loads = [
        pltpu.make_async_copy(offs_in, offs, l_sem.at[0]),
        pltpu.make_async_copy(kinds_in, kinds, l_sem.at[1]),
        pltpu.make_async_copy(mass_in, mass, l_sem.at[2]),
        pltpu.make_async_copy(basis, ub, l_sem.at[3]),
    ]
    for cp in loads:
        cp.start()
    near = jnp.where(edge, 2, 3)
    pl.semaphore_wait(barrier, near * quart - 1 + n_sp - 1)

    def relay(stage):
        for dl in (1, -1):
            seen = lev - dl * (stage - 1)

            @pl.when((seen >= 0) & (seen < LEVELS) & (lev + dl >= 0) & (lev + dl < LEVELS))
            def _():
                signal(known.at[stage - 2], tm + dl * quart, sp)

    def learn(stage):
        for dl in (1, -1):

            @pl.when((lev + dl * stage >= 0) & (lev + dl * stage < LEVELS))
            def _():
                pl.semaphore_wait(known.at[stage - 2], 1)

    def send_level(ci, to_lev, first=0):
        v0, v1 = chunks[ci]

        def send(i, carry):
            to = to_lev * quart + lax.rem(place + i, quart)
            pltpu.make_async_remote_copy(
                snap.at[pl.ds(v0, v1 - v0), :, pl.ds(pl.multiple_of(to * pts, pts), pts)],
                recs[ci].at[tm], a_send.at[ci], a_recv.at[ci],
                device_id={"tm": to, "space": sp}, device_id_type=MESH,
            ).start()
            return carry

        lax.fori_loop(first, quart, send, 0, unroll=side <= 32)

    relay(2)
    for ci, (v0, v1) in enumerate(chunks):
        mine = snap.at[pl.ds(v0, v1 - v0), :, pl.ds(pl.multiple_of(tm * pts, pts), pts)]
        if ci == 0:
            send_level(ci, lev + inward)
            pl.when(jnp.logical_not(edge))(lambda: send_level(ci, lev - inward))
            send_level(ci, lev, 1)
            learn(2)
            relay(3)
            send_level(ci, lev + 2 * inward)
            learn(3)
            pl.when(edge)(lambda: send_level(ci, lev + 3 * inward))

            def tell(i, carry):
                signal(known.at[2], tm, lax.rem(sp + i, n_sp))
                return carry

            lax.fori_loop(1, n_sp, tell, 0, unroll=side <= 32)
        else:
            pl.when(edge)(lambda: send_level(ci, lev + 3 * inward))
            send_level(ci, lev + 2 * inward)
            send_level(ci, lev + inward)
            pl.when(jnp.logical_not(edge))(lambda: send_level(ci, lev - inward))
            send_level(ci, lev, 1)
        pltpu.make_async_copy(mine, recs[ci].at[tm], a_recv.at[ci]).start()

    loads[0].wait()
    row = lax.broadcasted_iota(jnp.int32, (blocks, record), 0)
    lag = lax.broadcasted_iota(jnp.int32, (blocks, record), 1)
    for b in range(blocks):
        lag = jnp.where(row == b, lag - offs[b], lag)
    inside = (lag >= 0) & (lag < NT)
    theta = jnp.clip(lag, 0, NT - 1).astype(F32) * (2.0 * math.pi / NT)
    c1, s1v = jnp.cos(theta), jnp.sin(theta)
    win = jnp.where(inside, (0.5 - 0.5 * c1) * (1.0 / math.sqrt(0.375 * NT)), 0.0)
    cc, ss = win, jnp.zeros_like(win)
    for g, nf in enumerate(counts):
        parts = []
        for _ in range(nf):
            parts.append((cc, -ss))
            cc, ss = cc * c1 - ss * s1v, ss * c1 + cc * s1v
        table[g * lanes : g * lanes + 2 * nf * blocks] = jnp.concatenate(
            [p[c] for c in range(2) for p in parts], axis=0
        ).astype(BF)

    loads[1].wait()
    loads[2].wait()
    size = mass.shape[1]
    elems = pts // size
    strips = []
    for e in range(elems):
        kind = jnp.full((size, size), kinds[e], jnp.int32)
        blk = mass[0]
        for k in range(1, mass.shape[0]):
            blk = jnp.where(kind == k, mass[k], blk)
        zero = jnp.zeros_like(blk)
        strips.append(jnp.concatenate([blk if j == e else zero for j in range(elems)], axis=1))
    m_all = jnp.concatenate(strips, axis=0)
    m_hi = m_all.astype(BF)
    m_lo = (m_all - m_hi.astype(F32)).astype(BF)
    m_stack = jnp.concatenate([m_hi, m_hi, m_lo], axis=0)

    loads[3].wait()
    def fold(full, nf, rows):
        mask = freq_mask(nf, rows, lanes, blocks)
        real, imag = [
            jnp.sum(jnp.where(mask, part.reshape(nf, rows, lanes), 0.0), axis=0)
            for part in (full[: nf * rows], full[nf * rows :])
        ]
        imag = swap_halves(imag, nf * blocks)
        lane = lax.broadcasted_iota(jnp.int32, (rows, lanes), 1)
        return real + jnp.where(lane < nf * blocks, imag, -imag)

    coefs, grams = [None] * groups, [None] * groups
    for ci, (v0, v1) in enumerate(chunks):
        rec = recs[ci]
        pltpu.make_async_copy(rec, rec, a_recv.at[ci]).wait()
        count = v1 - v0
        x = jnp.concatenate([rec[:, v].reshape(record, pts) for v in range(count)], axis=1)
        spec = mm(table[...], x, ((1,), (0,)))
        s_hi = spec.astype(BF)
        s_lo = (spec - s_hi.astype(F32)).astype(BF)
        sh[:, v0 * pts : v1 * pts] = s_hi
        wts = []
        for v in range(count):
            cut = slice(v * pts, (v + 1) * pts)
            lhs = jnp.concatenate([s_hi[:, cut], s_lo[:, cut], s_hi[:, cut]], axis=1)
            wts.append(mm(lhs, m_stack, ((1,), (0,))).astype(BF))
        wt = jnp.concatenate(wts, axis=1)
        for g, nf in enumerate(counts):
            cut = slice(g * lanes, g * lanes + 2 * nf * blocks)
            f0 = g * GROUP
            u = [
                jnp.concatenate(
                    [ub[c, f0 : f0 + nf, v].reshape(nf * modes, pts) for v in range(v0, v1)], axis=1
                )
                for c in range(2)
            ]
            w = wt[cut]
            if w.shape[0] < lanes:
                w = jnp.concatenate([w, jnp.zeros((lanes - w.shape[0], w.shape[1]), BF)], axis=0)
            full = mm(jnp.concatenate(u + [s_hi[cut]], axis=0), w, ((1,), (1,)))
            coef = fold(full[: 2 * nf * modes], nf, modes) * scale
            gram = fold(full[2 * nf * modes :], nf, blocks)
            coefs[g] = coef if ci == 0 else coefs[g] + coef
            grams[g] = gram if ci == 0 else grams[g] + gram
    grams += [jnp.zeros_like(grams[0])] * (groups % 2)
    for at, tile in enumerate(
        coefs + [jnp.concatenate(grams[i : i + 2], axis=0) for i in range(0, groups, 2)]
    ):
        xb[at] = tile.astype(BF)

    pl.semaphore_wait(known.at[2], n_sp - 1)
    for o, (o_tm, o_sp) in enumerate(owners):

        @pl.when((tm != o_tm) | (sp != o_sp))
        def _():
            pltpu.make_async_remote_copy(
                xb.at[pl.ds(o * upo, upo)], plane.at[here], s1, r1,
                device_id={"tm": o_tm, "space": o_sp}, device_id_type=MESH,
            ).start()

    def wait_bytes(ref, sem):
        pltpu.make_async_copy(ref, ref, sem).wait()

    @pl.when(owner)
    def _():
        mine = pl.ds(spot * upo, upo)
        plane[here] = xb[mine]
        wait_bytes(plane.at[pl.ds(0, side - 1)], r1)
        yb[mine] = jnp.sum(plane[...].astype(F32), axis=0).astype(BF)

        def gather(i, carry):
            @pl.when(i != tm * n_sp + sp)
            def _():
                pltpu.make_async_remote_copy(
                    yb.at[mine], yb.at[mine], s2, r2,
                    device_id={"tm": lax.div(i, n_sp), "space": lax.rem(i, n_sp)}, device_id_type=MESH,
                ).start()

            return carry

        lax.fori_loop(0, side, gather, 0, unroll=side <= 32)
        wait_bytes(yb.at[pl.ds(0, (len(owners) - 1) * upo)], r2)

    @pl.when(jnp.logical_not(owner))
    def _():
        wait_bytes(yb, r2)

    y_out[...] = yb[...]
    for ci in range(len(chunks)):
        wait_bytes(recs[ci].at[pl.ds(0, n_tm - 1)], a_send.at[ci])

    @pl.when(owner)
    def _():
        wait_bytes(xb.at[pl.ds(0, (len(owners) - 1) * upo)], s1)
        wait_bytes(plane.at[pl.ds(0, side - 1)], s2)

    @pl.when(jnp.logical_not(owner))
    def _():
        wait_bytes(xb, s1)


def finish(entries, yb, sh, coef_out, new_out, ob, o_sem):
    freqs, nvar, modes, pts = new_out.shape[1:]
    blocks = coef_out.shape[1]
    lanes = yb.shape[2]
    groups = -(-freqs // GROUP)
    lane = lax.broadcasted_iota(jnp.int32, (modes, lanes), 1)
    lane_b = lane[:blocks]

    copies, tiles = [], []
    for g in range(groups):
        f0 = g * GROUP
        nf = min(GROUP, freqs - f0)
        half = nf * blocks

        def spread(val):
            rows = val.shape[0]
            big = jnp.broadcast_to(val[None], (nf, rows, lanes))
            return jnp.where(freq_mask(nf, rows, lanes, blocks), big, 0.0).reshape(nf * rows, lanes)

        coef = yb[g].astype(F32)
        gram = yb[groups + g // 2].astype(F32)[g % 2 * blocks : (g % 2 + 1) * blocks]
        tiles.append(coef)
        vec = spread(jnp.where(lane < half, coef, -coef))
        turned = swap_halves(gram, half)
        quad = jnp.concatenate([spread(gram), spread(jnp.where(lane_b < half, -turned, turned))], axis=0)
        rows = [vec[:, : 2 * half].astype(BF), spread(swap_halves(coef, half))[:, : 2 * half].astype(BF)]
        energy = jnp.sum(vec * mm(rows[0], quad.astype(BF), ((1,), (0,))), axis=1, keepdims=True)
        factor = 1.0 / jnp.sqrt(energy / entries + 1e-06)
        s_g = sh[g * lanes : g * lanes + 2 * half]
        for c in range(2):
            field = mm(rows[c], s_g, ((1,), (0,)))
            for v in range(nvar):
                val = (field[:, v * pts : (v + 1) * pts] * factor).astype(BF)
                ob[c, f0 : f0 + nf, v] = val.reshape(nf, modes, pts)
        cp = pltpu.make_async_copy(ob.at[:, pl.ds(f0, nf)], new_out.at[:, pl.ds(f0, nf)], o_sem.at[g])
        cp.start()
        copies.append(cp)

    row_b = lax.broadcasted_iota(jnp.int32, (blocks, modes, lanes), 0)
    pick = row_b == lax.broadcasted_iota(jnp.int32, (blocks, modes, lanes), 2) % blocks
    picked = [
        jnp.where(pick, jnp.broadcast_to(t[None], pick.shape), 0.0).reshape(blocks * modes, lanes)
        for t in tiles
    ]
    lhs = jnp.concatenate(picked, axis=1).astype(BF)
    row = lax.broadcasted_iota(jnp.int32, (lanes, freqs), 0)
    col = lax.broadcasted_iota(jnp.int32, (lanes, freqs), 1)
    for c in range(2):
        moves = []
        for g in range(groups):
            half = min(GROUP, freqs - g * GROUP) * blocks
            hit = (row // half == c) & (col == row % half // blocks + g * GROUP)
            moves.append(jnp.where(hit, 1.0, 0.0).astype(BF))
        moved = mm(lhs, jnp.concatenate(moves, axis=0), ((1,), (0,)))
        coef_out[c] = moved.reshape(blocks, modes, freqs)
    for cp in copies:
        cp.wait()


def solution(mesh):
    n_tm, n_sp = mesh.shape["tm"], mesh.shape["space"]
    n = n_tm * n_sp

    def on_device(snapshots, basis, mass_table, elem_kind, offsets):
        rows, nvar, slab = snapshots.shape
        _, freqs, modes, _, pts = basis.shape
        blocks = offsets.shape[0]
        groups = -(-freqs // GROUP)
        entries = nvar * pts * n
        pairs = groups + -(-groups // 2)
        side = n_tm * n_sp
        upo = -(-pairs // side)
        owners = owner_list(n_tm, n_sp, -(-pairs // upo))
        table_rows = 2 * freqs * blocks
        unit = (2 * blocks, 2 * GROUP * blocks)
        chunks = tuple((v, min(v + 2, nvar)) for v in range(0, nvar, 2))
        snap = jnp.transpose(snapshots, (1, 0, 2))
        base = jnp.transpose(basis, (0, 1, 3, 2, 4))
        hbm = pl.BlockSpec(memory_space=pltpu.HBM)
        vmem = pl.BlockSpec(memory_space=pltpu.VMEM)
        spec, total = pl.pallas_call(
            functools.partial(kernel, n_tm, n_sp, owners, entries, chunks),
            out_shape=(
                jax.ShapeDtypeStruct((table_rows, nvar * pts), BF),
                jax.ShapeDtypeStruct((len(owners) * upo,) + unit, BF),
            ),
            in_specs=[hbm] * 5,
            out_specs=(vmem, vmem),
            scratch_shapes=[
                pltpu.VMEM((table_rows, rows * n_tm), BF),
                pltpu.VMEM((2, freqs, nvar, modes, pts), BF),
                pltpu.VMEM((len(owners) * upo,) + unit, BF),
                pltpu.VMEM((side, upo) + unit, BF),
                pltpu.VMEM((len(owners) * upo,) + unit, BF),
                pltpu.VMEM(mass_table.shape, F32),
                pltpu.SMEM(elem_kind.shape, jnp.int32),
                pltpu.SMEM(offsets.shape, jnp.int32),
            ]
            + [pltpu.VMEM((n_tm, v1 - v0, rows, pts), BF) for v0, v1 in chunks]
            + [
                pltpu.SemaphoreType.DMA((len(chunks),)),
                pltpu.SemaphoreType.DMA((len(chunks),)),
                pltpu.SemaphoreType.DMA((4,)),
                pltpu.SemaphoreType.REGULAR((3,)),
            ]
            + [pltpu.SemaphoreType.DMA] * 4,
            compiler_params=pltpu.CompilerParams(
                collective_id=0, has_side_effects=True, vmem_limit_bytes=48 * 1024 * 1024
            ),
        )(*[pltpu.with_memory_space_constraint(a, pltpu.HBM) for a in (snap, base, mass_table, elem_kind, offsets)])
        coef, new = pl.pallas_call(
            functools.partial(finish, entries),
            out_shape=(
                jax.ShapeDtypeStruct((2, blocks, modes, freqs), F32),
                jax.ShapeDtypeStruct(base.shape, BF),
            ),
            in_specs=[vmem, vmem],
            out_specs=(vmem, hbm),
            scratch_shapes=[pltpu.VMEM(base.shape, BF), pltpu.SemaphoreType.DMA((groups,))],
            compiler_params=pltpu.CompilerParams(vmem_limit_bytes=32 * 1024 * 1024),
        )(total, spec)
        return jnp.transpose(coef, (0, 3, 1, 2)), jnp.transpose(new, (0, 1, 3, 2, 4))

    return jax.shard_map(
        on_device,
        mesh=mesh,
        in_specs=(
            P("tm", None, "space"),
            P(None, None, None, None, ("space", "tm")),
            P(),
            P(("space", "tm")),
            P(),
        ),
        out_specs=(P(), P(None, None, None, None, ("space", "tm"))),
        check_vma=False,
    )
```

```python
import functools
import math

import jax
import jax.numpy as jnp
from jax import lax
from jax.experimental import pallas as pl
from jax.experimental.pallas import tpu as pltpu
from jax.sharding import PartitionSpec as P

NT = 256
GROUP = 8
LEVELS = 4
MESH = pl.DeviceIdType.MESH
BF = jnp.bfloat16
F32 = jnp.float32


def owner_list(n_tm, n_sp, count):
    quart = n_tm // LEVELS
    first = [(quart, 0), (2 * quart, 0), (quart + 2, 0), (quart, 1)]
    spots = [(t + c, s) for t, s in first for c in range(2)]
    spots += [(t, s) for s in range(n_sp) for t in range(n_tm) if (t, s) not in spots]
    return tuple(p for p in spots if p[0] < n_tm and p[1] < n_sp)[:count]


def mm(a, b, contract):
    return lax.dot_general(a, b, (contract, ((), ())), preferred_element_type=F32)


def swap_halves(x, half):
    lanes = x.shape[1]
    if 2 * half == lanes:
        return pltpu.roll(x, half, 1)
    lane = lax.broadcasted_iota(jnp.int32, x.shape, 1)
    return jnp.where(lane < half, pltpu.roll(x, lanes - half, 1), pltpu.roll(x, half, 1))


def freq_mask(nf, rows, lanes, blocks):
    row_f = lax.broadcasted_iota(jnp.int32, (nf, rows, lanes), 0)
    lane = lax.broadcasted_iota(jnp.int32, (nf, rows, lanes), 2)
    half = nf * blocks
    return (row_f == lane % half // blocks) & (lane < 2 * half)


def kernel(
    n_tm, n_sp, owners, entries, chunks,
    snap, basis, mass_in, kinds_in, offs_in,
    sh, y_out,
    table, ub, xb, plane, yb, mass, kinds, offs, *rest,
):
    recs, (a_send, a_recv, l_sem, known, s1, r1, s2, r2) = rest[: len(chunks)], rest[len(chunks) :]
    tm = lax.axis_index("tm")
    sp = lax.axis_index("space")
    side = n_tm * n_sp
    scale = 1.0 / math.sqrt(entries)
    here = sp * n_tm + tm
    is_own = [(tm == o_tm) & (sp == o_sp) for o_tm, o_sp in owners]
    owner = functools.reduce(jnp.logical_or, is_own)
    spot = sum(jnp.where(m, o, 0) for o, m in enumerate(is_own))
    quart = n_tm // LEVELS
    lev, place = lax.div(tm, quart), lax.rem(tm, quart)
    edge = (lev == 0) | (lev == LEVELS - 1)
    inward = jnp.where(lev < LEVELS // 2, 1, -1)
    freqs = basis.shape[1]
    rows, pts = recs[0].shape[2:]
    groups = -(-freqs // GROUP)
    counts = [min(GROUP, freqs - g * GROUP) for g in range(groups)]
    record = n_tm * rows
    blocks = offs.shape[0]
    modes = basis.shape[3]
    upo = plane.shape[1]
    lanes = 2 * GROUP * blocks

    barrier = pltpu.get_barrier_semaphore()

    def signal(sem, to_tm, to_sp):
        pl.semaphore_signal(
            sem, inc=1, device_id={"tm": to_tm, "space": to_sp}, device_id_type=MESH
        )

    for dl in (1, -1, 0):

        def greet(i, carry):
            to = (lev + dl) * quart + lax.rem(place + i, quart)
            signal(barrier, to, sp)
            return carry

        @pl.when((lev + dl >= 0) & (lev + dl < LEVELS))
        def _():
            lax.fori_loop(1 if dl == 0 else 0, quart, greet, 0, unroll=side <= 32)

    def greet_side(i, carry):
        signal(barrier, tm, lax.rem(sp + i, n_sp))
        return carry

    lax.fori_loop(1, n_sp, greet_side, 0, unroll=side <= 32)
    loads = [
        pltpu.make_async_copy(offs_in, offs, l_sem.at[0]),
        pltpu.make_async_copy(kinds_in, kinds, l_sem.at[1]),
        pltpu.make_async_copy(mass_in, mass, l_sem.at[2]),
        pltpu.make_async_copy(basis, ub, l_sem.at[3]),
    ]
    for cp in loads:
        cp.start()
    near = jnp.where(edge, 2, 3)
    pl.semaphore_wait(barrier, near * quart - 1 + n_sp - 1)

    def relay(stage):
        for dl in (1, -1):
            seen = lev - dl * (stage - 1)

            @pl.when((seen >= 0) & (seen < LEVELS) & (lev + dl >= 0) & (lev + dl < LEVELS))
            def _():
                signal(known.at[stage - 2], tm + dl * quart, sp)

    def learn(stage):
        for dl in (1, -1):

            @pl.when((lev + dl * stage >= 0) & (lev + dl * stage < LEVELS))
            def _():
                pl.semaphore_wait(known.at[stage - 2], 1)

    def send_level(ci, to_lev, first=0):
        v0, v1 = chunks[ci]

        def send(i, carry):
            to = to_lev * quart + lax.rem(place + i, quart)
            pltpu.make_async_remote_copy(
                snap.at[pl.ds(v0, v1 - v0), :, pl.ds(pl.multiple_of(to * pts, pts), pts)],
                recs[ci].at[tm], a_send.at[ci], a_recv.at[ci],
                device_id={"tm": to, "space": sp}, device_id_type=MESH,
            ).start()
            return carry

        lax.fori_loop(first, quart, send, 0, unroll=side <= 32)

    relay(2)
    for ci, (v0, v1) in enumerate(chunks):
        mine = snap.at[pl.ds(v0, v1 - v0), :, pl.ds(pl.multiple_of(tm * pts, pts), pts)]
        if ci == 0:
            send_level(ci, lev + inward)
            pl.when(jnp.logical_not(edge))(lambda: send_level(ci, lev - inward))
            send_level(ci, lev, 1)
            learn(2)
            relay(3)
            send_level(ci, lev + 2 * inward)
            learn(3)
            pl.when(edge)(lambda: send_level(ci, lev + 3 * inward))

            def tell(i, carry):
                signal(known.at[2], tm, lax.rem(sp + i, n_sp))
                return carry

            lax.fori_loop(1, n_sp, tell, 0, unroll=side <= 32)
        else:
            pl.when(edge)(lambda: send_level(ci, lev + 3 * inward))
            send_level(ci, lev + 2 * inward)
            send_level(ci, lev + inward)
            pl.when(jnp.logical_not(edge))(lambda: send_level(ci, lev - inward))
            send_level(ci, lev, 1)
        pltpu.make_async_copy(mine, recs[ci].at[tm], a_recv.at[ci]).start()

    loads[0].wait()
    row = lax.broadcasted_iota(jnp.int32, (blocks, record), 0)
    lag = lax.broadcasted_iota(jnp.int32, (blocks, record), 1)
    for b in range(blocks):
        lag = jnp.where(row == b, lag - offs[b], lag)
    inside = (lag >= 0) & (lag < NT)
    theta = jnp.clip(lag, 0, NT - 1).astype(F32) * (2.0 * math.pi / NT)
    c1, s1v = jnp.cos(theta), jnp.sin(theta)
    win = jnp.where(inside, (0.5 - 0.5 * c1) * (1.0 / math.sqrt(0.375 * NT)), 0.0)
    cc, ss = win, jnp.zeros_like(win)
    for g, nf in enumerate(counts):
        parts = []
        for _ in range(nf):
            parts.append((cc, -ss))
            cc, ss = cc * c1 - ss * s1v, ss * c1 + cc * s1v
        table[g * lanes : g * lanes + 2 * nf * blocks] = jnp.concatenate(
            [p[c] for c in range(2) for p in parts], axis=0
        ).astype(BF)

    loads[1].wait()
    loads[2].wait()
    size = mass.shape[1]
    elems = pts // size
    strips = []
    for e in range(elems):
        kind = jnp.full((size, size), kinds[e], jnp.int32)
        blk = mass[0]
        for k in range(1, mass.shape[0]):
            blk = jnp.where(kind == k, mass[k], blk)
        zero = jnp.zeros_like(blk)
        strips.append(jnp.concatenate([blk if j == e else zero for j in range(elems)], axis=1))
    m_all = jnp.concatenate(strips, axis=0)
    m_hi = m_all.astype(BF)
    m_lo = (m_all - m_hi.astype(F32)).astype(BF)
    m_stack = jnp.concatenate([m_hi, m_hi, m_lo], axis=0)

    loads[3].wait()
    def fold(full, nf, rows):
        mask = freq_mask(nf, rows, lanes, blocks)
        real, imag = [
            jnp.sum(jnp.where(mask, part.reshape(nf, rows, lanes), 0.0), axis=0)
            for part in (full[: nf * rows], full[nf * rows :])
        ]
        imag = swap_halves(imag, nf * blocks)
        lane = lax.broadcasted_iota(jnp.int32, (rows, lanes), 1)
        return real + jnp.where(lane < nf * blocks, imag, -imag)

    coefs, grams = [None] * groups, [None] * groups
    for ci, (v0, v1) in enumerate(chunks):
        rec = recs[ci]
        pltpu.make_async_copy(rec, rec, a_recv.at[ci]).wait()
        count = v1 - v0
        x = jnp.concatenate([rec[:, v].reshape(record, pts) for v in range(count)], axis=1)
        spec = mm(table[...], x, ((1,), (0,)))
        s_hi = spec.astype(BF)
        s_lo = (spec - s_hi.astype(F32)).astype(BF)
        sh[:, v0 * pts : v1 * pts] = s_hi
        wts = []
        for v in range(count):
            cut = slice(v * pts, (v + 1) * pts)
            lhs = jnp.concatenate([s_hi[:, cut], s_lo[:, cut], s_hi[:, cut]], axis=1)
            wts.append(mm(lhs, m_stack, ((1,), (0,))).astype(BF))
        wt = jnp.concatenate(wts, axis=1)
        for g, nf in enumerate(counts):
            cut = slice(g * lanes, g * lanes + 2 * nf * blocks)
            f0 = g * GROUP
            u = [
                jnp.concatenate(
                    [ub[c, f0 : f0 + nf, v].reshape(nf * modes, pts) for v in range(v0, v1)], axis=1
                )
                for c in range(2)
            ]
            w = wt[cut]
            if w.shape[0] < lanes:
                w = jnp.concatenate([w, jnp.zeros((lanes - w.shape[0], w.shape[1]), BF)], axis=0)
            full = mm(jnp.concatenate(u + [s_hi[cut]], axis=0), w, ((1,), (1,)))
            coef = fold(full[: 2 * nf * modes], nf, modes) * scale
            gram = fold(full[2 * nf * modes :], nf, blocks)
            coefs[g] = coef if ci == 0 else coefs[g] + coef
            grams[g] = gram if ci == 0 else grams[g] + gram
    grams += [jnp.zeros_like(grams[0])] * (groups % 2)
    for at, tile in enumerate(
        coefs + [jnp.concatenate(grams[i : i + 2], axis=0) for i in range(0, groups, 2)]
    ):
        xb[at] = tile.astype(BF)

    pl.semaphore_wait(known.at[2], n_sp - 1)
    for o, (o_tm, o_sp) in enumerate(owners):

        @pl.when((tm != o_tm) | (sp != o_sp))
        def _():
            pltpu.make_async_remote_copy(
                xb.at[pl.ds(o * upo, upo)], plane.at[here], s1, r1,
                device_id={"tm": o_tm, "space": o_sp}, device_id_type=MESH,
            ).start()

    def wait_bytes(ref, sem):
        pltpu.make_async_copy(ref, ref, sem).wait()

    @pl.when(owner)
    def _():
        mine = pl.ds(spot * upo, upo)
        plane[here] = xb[mine]
        wait_bytes(plane.at[pl.ds(0, side - 1)], r1)
        yb[mine] = jnp.sum(plane[...].astype(F32), axis=0).astype(BF)

        def gather(i, carry):
            @pl.when(i != tm * n_sp + sp)
            def _():
                pltpu.make_async_remote_copy(
                    yb.at[mine], yb.at[mine], s2, r2,
                    device_id={"tm": lax.div(i, n_sp), "space": lax.rem(i, n_sp)}, device_id_type=MESH,
                ).start()

            return carry

        lax.fori_loop(0, side, gather, 0, unroll=side <= 32)
        wait_bytes(yb.at[pl.ds(0, (len(owners) - 1) * upo)], r2)

    @pl.when(jnp.logical_not(owner))
    def _():
        wait_bytes(yb, r2)

    y_out[...] = yb[...]
    for ci in range(len(chunks)):
        wait_bytes(recs[ci].at[pl.ds(0, n_tm - 1)], a_send.at[ci])

    @pl.when(owner)
    def _():
        wait_bytes(xb.at[pl.ds(0, (len(owners) - 1) * upo)], s1)
        wait_bytes(plane.at[pl.ds(0, side - 1)], s2)

    @pl.when(jnp.logical_not(owner))
    def _():
        wait_bytes(xb, s1)


def finish(entries, yb, sh, coef_hbm, new_out, ob, coef_out, o_sem):
    freqs, nvar, modes, pts = new_out.shape[1:]
    blocks = coef_out.shape[1]
    lanes = yb.shape[2]
    groups = -(-freqs // GROUP)
    lane = lax.broadcasted_iota(jnp.int32, (modes, lanes), 1)
    lane_b = lane[:blocks]

    copies, tiles = [], [yb[g].astype(F32) for g in range(groups)]
    row_b = lax.broadcasted_iota(jnp.int32, (blocks, modes, lanes), 0)
    pick = row_b == lax.broadcasted_iota(jnp.int32, (blocks, modes, lanes), 2) % blocks
    picked = [
        jnp.where(pick, jnp.broadcast_to(t[None], pick.shape), 0.0).reshape(blocks * modes, lanes)
        for t in tiles
    ]
    lhs = jnp.concatenate(picked, axis=1).astype(BF)
    row = lax.broadcasted_iota(jnp.int32, (lanes, freqs), 0)
    col = lax.broadcasted_iota(jnp.int32, (lanes, freqs), 1)
    for c in range(2):
        moves = []
        for g in range(groups):
            half = min(GROUP, freqs - g * GROUP) * blocks
            hit = (row // half == c) & (col == row % half // blocks + g * GROUP)
            moves.append(jnp.where(hit, 1.0, 0.0).astype(BF))
        moved = mm(lhs, jnp.concatenate(moves, axis=0), ((1,), (0,)))
        coef_out[c] = moved.reshape(blocks, modes, freqs)
    cp = pltpu.make_async_copy(coef_out, coef_hbm, o_sem.at[groups])
    cp.start()
    copies.append(cp)

    for g in range(groups):
        f0 = g * GROUP
        nf = min(GROUP, freqs - f0)
        half = nf * blocks

        def spread(val):
            rows = val.shape[0]
            big = jnp.broadcast_to(val[None], (nf, rows, lanes))
            return jnp.where(freq_mask(nf, rows, lanes, blocks), big, 0.0).reshape(nf * rows, lanes)

        coef = tiles[g]
        gram = yb[groups + g // 2].astype(F32)[g % 2 * blocks : (g % 2 + 1) * blocks]
        vec = spread(jnp.where(lane < half, coef, -coef))
        turned = swap_halves(gram, half)
        quad = jnp.concatenate([spread(gram), spread(jnp.where(lane_b < half, -turned, turned))], axis=0)
        rows = [vec[:, : 2 * half].astype(BF), spread(swap_halves(coef, half))[:, : 2 * half].astype(BF)]
        energy = jnp.sum(vec * mm(rows[0], quad.astype(BF), ((1,), (0,))), axis=1, keepdims=True)
        factor = 1.0 / jnp.sqrt(energy / entries + 1e-06)
        s_g = sh[g * lanes : g * lanes + 2 * half]
        for c in range(2):
            field = mm(rows[c], s_g, ((1,), (0,)))
            for v in range(nvar):
                val = (field[:, v * pts : (v + 1) * pts] * factor).astype(BF)
                ob[c, f0 : f0 + nf, v] = val.reshape(nf, modes, pts)
        cp = pltpu.make_async_copy(ob.at[:, pl.ds(f0, nf)], new_out.at[:, pl.ds(f0, nf)], o_sem.at[g])
        cp.start()
        copies.append(cp)

    for cp in copies:
        cp.wait()


def solution(mesh):
    n_tm, n_sp = mesh.shape["tm"], mesh.shape["space"]
    n = n_tm * n_sp

    def on_device(snapshots, basis, mass_table, elem_kind, offsets):
        rows, nvar, slab = snapshots.shape
        _, freqs, modes, _, pts = basis.shape
        blocks = offsets.shape[0]
        groups = -(-freqs // GROUP)
        entries = nvar * pts * n
        pairs = groups + -(-groups // 2)
        side = n_tm * n_sp
        upo = -(-pairs // side)
        owners = owner_list(n_tm, n_sp, -(-pairs // upo))
        table_rows = 2 * freqs * blocks
        unit = (2 * blocks, 2 * GROUP * blocks)
        chunks = tuple((v, min(v + 2, nvar)) for v in range(0, nvar, 2))
        snap = jnp.transpose(snapshots, (1, 0, 2))
        base = jnp.transpose(basis, (0, 1, 3, 2, 4))
        hbm = pl.BlockSpec(memory_space=pltpu.HBM)
        vmem = pl.BlockSpec(memory_space=pltpu.VMEM)
        spec, total = pl.pallas_call(
            functools.partial(kernel, n_tm, n_sp, owners, entries, chunks),
            out_shape=(
                jax.ShapeDtypeStruct((table_rows, nvar * pts), BF),
                jax.ShapeDtypeStruct((len(owners) * upo,) + unit, BF),
            ),
            in_specs=[hbm] * 5,
            out_specs=(vmem, vmem),
            scratch_shapes=[
                pltpu.VMEM((table_rows, rows * n_tm), BF),
                pltpu.VMEM((2, freqs, nvar, modes, pts), BF),
                pltpu.VMEM((len(owners) * upo,) + unit, BF),
                pltpu.VMEM((side, upo) + unit, BF),
                pltpu.VMEM((len(owners) * upo,) + unit, BF),
                pltpu.VMEM(mass_table.shape, F32),
                pltpu.SMEM(elem_kind.shape, jnp.int32),
                pltpu.SMEM(offsets.shape, jnp.int32),
            ]
            + [pltpu.VMEM((n_tm, v1 - v0, rows, pts), BF) for v0, v1 in chunks]
            + [
                pltpu.SemaphoreType.DMA((len(chunks),)),
                pltpu.SemaphoreType.DMA((len(chunks),)),
                pltpu.SemaphoreType.DMA((4,)),
                pltpu.SemaphoreType.REGULAR((3,)),
            ]
            + [pltpu.SemaphoreType.DMA] * 4,
            compiler_params=pltpu.CompilerParams(
                collective_id=0, has_side_effects=True, vmem_limit_bytes=48 * 1024 * 1024
            ),
        )(*[pltpu.with_memory_space_constraint(a, pltpu.HBM) for a in (snap, base, mass_table, elem_kind, offsets)])
        coef, new = pl.pallas_call(
            functools.partial(finish, entries),
            out_shape=(
                jax.ShapeDtypeStruct((2, blocks, modes, freqs), F32),
                jax.ShapeDtypeStruct(base.shape, BF),
            ),
            in_specs=[vmem, vmem],
            out_specs=(hbm, hbm),
            scratch_shapes=[
                pltpu.VMEM(base.shape, BF),
                pltpu.VMEM((2, blocks, modes, freqs), F32),
                pltpu.SemaphoreType.DMA((groups + 1,)),
            ],
            compiler_params=pltpu.CompilerParams(vmem_limit_bytes=32 * 1024 * 1024),
        )(total, spec)
        return jnp.transpose(coef, (0, 3, 1, 2)), jnp.transpose(new, (0, 1, 3, 2, 4))

    return jax.shard_map(
        on_device,
        mesh=mesh,
        in_specs=(
            P("tm", None, "space"),
            P(None, None, None, None, ("space", "tm")),
            P(),
            P(("space", "tm")),
            P(),
        ),
        out_specs=(P(), P(None, None, None, None, ("space", "tm"))),
        check_vma=False,
    )
```

```python
import functools
import math

import jax
import jax.numpy as jnp
from jax import lax
from jax.experimental import pallas as pl
from jax.experimental.pallas import tpu as pltpu
from jax.sharding import PartitionSpec as P

NT = 256
GROUP = 8
LEVELS = 4
MESH = pl.DeviceIdType.MESH
BF = jnp.bfloat16
F32 = jnp.float32


def owner_list(n_tm, n_sp, count):
    quart = n_tm // LEVELS
    spots = [(t % n_tm, s) for t in range(quart, quart + n_tm, 2) for s in range(n_sp)]
    spots = [(t + c, s) for t, s in spots for c in range(2)]
    return tuple(spots[:count])


def mm(a, b, contract):
    return lax.dot_general(a, b, (contract, ((), ())), preferred_element_type=F32)


def swap_halves(x, half):
    lanes = x.shape[1]
    if 2 * half == lanes:
        return pltpu.roll(x, half, 1)
    lane = lax.broadcasted_iota(jnp.int32, x.shape, 1)
    return jnp.where(lane < half, pltpu.roll(x, lanes - half, 1), pltpu.roll(x, half, 1))


def freq_mask(nf, rows, lanes, blocks):
    row_f = lax.broadcasted_iota(jnp.int32, (nf, rows, lanes), 0)
    lane = lax.broadcasted_iota(jnp.int32, (nf, rows, lanes), 2)
    half = nf * blocks
    return (row_f == lane % half // blocks) & (lane < 2 * half)


def kernel(
    n_tm, n_sp, owners, entries, chunks,
    snap, basis, mass_in, kinds_in, offs_in,
    sh, y_out,
    table, ub, xb, plane, yb, mass, kinds, offs, *rest,
):
    recs, (a_send, a_recv, l_sem, known, s1, r1, s2, r2) = rest[: len(chunks)], rest[len(chunks) :]
    tm = lax.axis_index("tm")
    sp = lax.axis_index("space")
    side = n_tm * n_sp
    scale = 1.0 / math.sqrt(entries)
    here = sp * n_tm + tm
    is_own = [(tm == o_tm) & (sp == o_sp) for o_tm, o_sp in owners]
    owner = functools.reduce(jnp.logical_or, is_own)
    spot = sum(jnp.where(m, o, 0) for o, m in enumerate(is_own))
    quart = n_tm // LEVELS
    lev, place = lax.div(tm, quart), lax.rem(tm, quart)
    edge = (lev == 0) | (lev == LEVELS - 1)
    inward = jnp.where(lev < LEVELS // 2, 1, -1)
    freqs = basis.shape[1]
    rows, pts = recs[0].shape[2:]
    groups = -(-freqs // GROUP)
    counts = [min(GROUP, freqs - g * GROUP) for g in range(groups)]
    record = n_tm * rows
    blocks = offs.shape[0]
    modes = basis.shape[3]
    upo = plane.shape[1]
    lanes = 2 * GROUP * blocks

    barrier = pltpu.get_barrier_semaphore()

    def signal(sem, to_tm, to_sp):
        pl.semaphore_signal(
            sem, inc=1, device_id={"tm": to_tm, "space": to_sp}, device_id_type=MESH
        )

    for dl in (1, -1, 0):

        def greet(i, carry):
            to = (lev + dl) * quart + lax.rem(place + i, quart)
            signal(barrier, to, sp)
            return carry

        @pl.when((lev + dl >= 0) & (lev + dl < LEVELS))
        def _():
            lax.fori_loop(1 if dl == 0 else 0, quart, greet, 0, unroll=side <= 32)

    def greet_side(i, carry):
        signal(barrier, tm, lax.rem(sp + i, n_sp))
        return carry

    lax.fori_loop(1, n_sp, greet_side, 0, unroll=side <= 32)
    loads = [
        pltpu.make_async_copy(offs_in, offs, l_sem.at[0]),
        pltpu.make_async_copy(kinds_in, kinds, l_sem.at[1]),
        pltpu.make_async_copy(mass_in, mass, l_sem.at[2]),
        pltpu.make_async_copy(basis, ub, l_sem.at[3]),
    ]
    for cp in loads:
        cp.start()
    near = jnp.where(edge, 2, 3)
    pl.semaphore_wait(barrier, near * quart - 1 + n_sp - 1)

    def relay(stage):
        for dl in (1, -1):
            seen = lev - dl * (stage - 1)

            @pl.when((seen >= 0) & (seen < LEVELS) & (lev + dl >= 0) & (lev + dl < LEVELS))
            def _():
                signal(known.at[stage - 2], tm + dl * quart, sp)

    def learn(stage):
        for dl in (1, -1):

            @pl.when((lev + dl * stage >= 0) & (lev + dl * stage < LEVELS))
            def _():
                pl.semaphore_wait(known.at[stage - 2], 1)

    def send_level(ci, to_lev, first=0):
        v0, v1 = chunks[ci]

        def send(i, carry):
            to = to_lev * quart + lax.rem(place + i, quart)
            pltpu.make_async_remote_copy(
                snap.at[pl.ds(v0, v1 - v0), :, pl.ds(pl.multiple_of(to * pts, pts), pts)],
                recs[ci].at[tm], a_send.at[ci], a_recv.at[ci],
                device_id={"tm": to, "space": sp}, device_id_type=MESH,
            ).start()
            return carry

        lax.fori_loop(first, quart, send, 0, unroll=side <= 32)

    relay(2)
    for ci, (v0, v1) in enumerate(chunks):
        mine = snap.at[pl.ds(v0, v1 - v0), :, pl.ds(pl.multiple_of(tm * pts, pts), pts)]
        if ci == 0:
            send_level(ci, lev + inward)
            pl.when(jnp.logical_not(edge))(lambda: send_level(ci, lev - inward))
            send_level(ci, lev, 1)
            learn(2)
            relay(3)
            send_level(ci, lev + 2 * inward)
            learn(3)
            pl.when(edge)(lambda: send_level(ci, lev + 3 * inward))

            def tell(i, carry):
                signal(known.at[2], tm, lax.rem(sp + i, n_sp))
                return carry

            lax.fori_loop(1, n_sp, tell, 0, unroll=side <= 32)
        else:
            pl.when(edge)(lambda: send_level(ci, lev + 3 * inward))
            send_level(ci, lev + 2 * inward)
            send_level(ci, lev + inward)
            pl.when(jnp.logical_not(edge))(lambda: send_level(ci, lev - inward))
            send_level(ci, lev, 1)
        pltpu.make_async_copy(mine, recs[ci].at[tm], a_recv.at[ci]).start()

    loads[0].wait()
    row = lax.broadcasted_iota(jnp.int32, (blocks, record), 0)
    lag = lax.broadcasted_iota(jnp.int32, (blocks, record), 1)
    for b in range(blocks):
        lag = jnp.where(row == b, lag - offs[b], lag)
    inside = (lag >= 0) & (lag < NT)
    theta = jnp.clip(lag, 0, NT - 1).astype(F32) * (2.0 * math.pi / NT)
    c1, s1v = jnp.cos(theta), jnp.sin(theta)
    win = jnp.where(inside, (0.5 - 0.5 * c1) * (1.0 / math.sqrt(0.375 * NT)), 0.0)
    cc, ss = win, jnp.zeros_like(win)
    for g, nf in enumerate(counts):
        parts = []
        for _ in range(nf):
            parts.append((cc, -ss))
            cc, ss = cc * c1 - ss * s1v, ss * c1 + cc * s1v
        table[g * lanes : g * lanes + 2 * nf * blocks] = jnp.concatenate(
            [p[c] for c in range(2) for p in parts], axis=0
        ).astype(BF)

    loads[1].wait()
    loads[2].wait()
    size = mass.shape[1]
    elems = pts // size
    strips = []
    for e in range(elems):
        kind = jnp.full((size, size), kinds[e], jnp.int32)
        blk = mass[0]
        for k in range(1, mass.shape[0]):
            blk = jnp.where(kind == k, mass[k], blk)
        zero = jnp.zeros_like(blk)
        strips.append(jnp.concatenate([blk if j == e else zero for j in range(elems)], axis=1))
    m_all = jnp.concatenate(strips, axis=0)
    m_hi = m_all.astype(BF)
    m_lo = (m_all - m_hi.astype(F32)).astype(BF)
    m_stack = jnp.concatenate([m_hi, m_hi, m_lo], axis=0)

    loads[3].wait()
    def fold(full, nf, rows):
        mask = freq_mask(nf, rows, lanes, blocks)
        real, imag = [
            jnp.sum(jnp.where(mask, part.reshape(nf, rows, lanes), 0.0), axis=0)
            for part in (full[: nf * rows], full[nf * rows :])
        ]
        imag = swap_halves(imag, nf * blocks)
        lane = lax.broadcasted_iota(jnp.int32, (rows, lanes), 1)
        return real + jnp.where(lane < nf * blocks, imag, -imag)

    coefs, grams = [None] * groups, [None] * groups
    for ci, (v0, v1) in enumerate(chunks):
        rec = recs[ci]
        pltpu.make_async_copy(rec, rec, a_recv.at[ci]).wait()
        count = v1 - v0
        x = jnp.concatenate([rec[:, v].reshape(record, pts) for v in range(count)], axis=1)
        cuts = [0, table.shape[0]] if count > 1 else [0, lanes * (groups // 2), table.shape[0]]
        spec = jnp.concatenate([mm(table[i:j], x, ((1,), (0,))) for i, j in zip(cuts, cuts[1:])], axis=0)
        s_hi = spec.astype(BF)
        s_lo = (spec - s_hi.astype(F32)).astype(BF)
        sh[:, v0 * pts : v1 * pts] = s_hi
        wts = []
        for v in range(count):
            cut = slice(v * pts, (v + 1) * pts)
            lhs = jnp.concatenate([s_hi[:, cut], s_lo[:, cut], s_hi[:, cut]], axis=1)
            wts.append(
                jnp.concatenate(
                    [mm(lhs[i:j], m_stack, ((1,), (0,))).astype(BF) for i, j in zip(cuts, cuts[1:])], axis=0
                )
            )
        wt = jnp.concatenate(wts, axis=1)
        for g, nf in enumerate(counts):
            cut = slice(g * lanes, g * lanes + 2 * nf * blocks)
            f0 = g * GROUP
            u = [
                jnp.concatenate(
                    [ub[c, f0 : f0 + nf, v].reshape(nf * modes, pts) for v in range(v0, v1)], axis=1
                )
                for c in range(2)
            ]
            w = wt[cut]
            if w.shape[0] < lanes:
                w = jnp.concatenate([w, jnp.zeros((lanes - w.shape[0], w.shape[1]), BF)], axis=0)
            full = mm(jnp.concatenate(u + [s_hi[cut]], axis=0), w, ((1,), (1,)))
            coef = fold(full[: 2 * nf * modes], nf, modes) * scale
            gram = fold(full[2 * nf * modes :], nf, blocks)
            coefs[g] = coef if ci == 0 else coefs[g] + coef
            grams[g] = gram if ci == 0 else grams[g] + gram
    grams += [jnp.zeros_like(grams[0])] * (groups % 2)
    for at, tile in enumerate(
        coefs + [jnp.concatenate(grams[i : i + 2], axis=0) for i in range(0, groups, 2)]
    ):
        xb[at] = tile.astype(BF)

    pl.semaphore_wait(known.at[2], n_sp - 1)
    for o, (o_tm, o_sp) in enumerate(owners):

        @pl.when((tm != o_tm) | (sp != o_sp))
        def _():
            pltpu.make_async_remote_copy(
                xb.at[pl.ds(o * upo, upo)], plane.at[here], s1, r1,
                device_id={"tm": o_tm, "space": o_sp}, device_id_type=MESH,
            ).start()

    def wait_bytes(ref, sem):
        pltpu.make_async_copy(ref, ref, sem).wait()

    @pl.when(owner)
    def _():
        mine = pl.ds(spot * upo, upo)
        plane[here] = xb[mine]
        wait_bytes(plane.at[pl.ds(0, side - 1)], r1)
        yb[mine] = jnp.sum(plane[...].astype(F32), axis=0).astype(BF)

        def gather(i, carry):
            @pl.when(i != tm * n_sp + sp)
            def _():
                pltpu.make_async_remote_copy(
                    yb.at[mine], yb.at[mine], s2, r2,
                    device_id={"tm": lax.div(i, n_sp), "space": lax.rem(i, n_sp)}, device_id_type=MESH,
                ).start()

            return carry

        lax.fori_loop(0, side, gather, 0, unroll=side <= 32)
        wait_bytes(yb.at[pl.ds(0, (len(owners) - 1) * upo)], r2)

    @pl.when(jnp.logical_not(owner))
    def _():
        wait_bytes(yb, r2)

    y_out[...] = yb[...]
    for ci in range(len(chunks)):
        wait_bytes(recs[ci].at[pl.ds(0, n_tm - 1)], a_send.at[ci])

    @pl.when(owner)
    def _():
        wait_bytes(xb.at[pl.ds(0, (len(owners) - 1) * upo)], s1)
        wait_bytes(plane.at[pl.ds(0, side - 1)], s2)

    @pl.when(jnp.logical_not(owner))
    def _():
        wait_bytes(xb, s1)


def finish(entries, yb, sh, coef_hbm, new_out, ob, coef_out, o_sem):
    freqs, nvar, modes, pts = new_out.shape[1:]
    blocks = coef_out.shape[1]
    lanes = yb.shape[2]
    groups = -(-freqs // GROUP)
    lane = lax.broadcasted_iota(jnp.int32, (modes, lanes), 1)
    lane_b = lane[:blocks]

    copies, tiles = [], [yb[g].astype(F32) for g in range(groups)]
    row_b = lax.broadcasted_iota(jnp.int32, (blocks, modes, lanes), 0)
    pick = row_b == lax.broadcasted_iota(jnp.int32, (blocks, modes, lanes), 2) % blocks
    picked = [
        jnp.where(pick, jnp.broadcast_to(t[None], pick.shape), 0.0).reshape(blocks * modes, lanes)
        for t in tiles
    ]
    lhs = jnp.concatenate(picked, axis=1).astype(BF)
    row = lax.broadcasted_iota(jnp.int32, (lanes, freqs), 0)
    col = lax.broadcasted_iota(jnp.int32, (lanes, freqs), 1)
    for c in range(2):
        moves = []
        for g in range(groups):
            half = min(GROUP, freqs - g * GROUP) * blocks
            hit = (row // half == c) & (col == row % half // blocks + g * GROUP)
            moves.append(jnp.where(hit, 1.0, 0.0).astype(BF))
        moved = mm(lhs, jnp.concatenate(moves, axis=0), ((1,), (0,)))
        coef_out[c] = moved.reshape(blocks, modes, freqs)
    cp = pltpu.make_async_copy(coef_out, coef_hbm, o_sem.at[groups])
    cp.start()
    copies.append(cp)

    for g in range(groups):
        f0 = g * GROUP
        nf = min(GROUP, freqs - f0)
        half = nf * blocks

        def spread(val):
            rows = val.shape[0]
            big = jnp.broadcast_to(val[None], (nf, rows, lanes))
            return jnp.where(freq_mask(nf, rows, lanes, blocks), big, 0.0).reshape(nf * rows, lanes)

        coef = tiles[g]
        gram = yb[groups + g // 2].astype(F32)[g % 2 * blocks : (g % 2 + 1) * blocks]
        vec = spread(jnp.where(lane < half, coef, -coef))
        turned = swap_halves(gram, half)
        quad = jnp.concatenate([spread(gram), spread(jnp.where(lane_b < half, -turned, turned))], axis=0)
        rows = [vec[:, : 2 * half].astype(BF), spread(swap_halves(coef, half))[:, : 2 * half].astype(BF)]
        energy = jnp.sum(vec * mm(rows[0], quad.astype(BF), ((1,), (0,))), axis=1, keepdims=True)
        factor = 1.0 / jnp.sqrt(energy / entries + 1e-06)
        both = jnp.concatenate(rows, axis=0)
        whole = mm(both, sh[g * lanes : g * lanes + 2 * half], ((1,), (0,)))
        for v in range(nvar):
            for c in range(2):
                val = (whole[c * nf * modes : (c + 1) * nf * modes, v * pts : (v + 1) * pts] * factor).astype(BF)
                ob[c, f0 : f0 + nf, v] = val.reshape(nf, modes, pts)
        cp = pltpu.make_async_copy(ob.at[:, pl.ds(f0, nf)], new_out.at[:, pl.ds(f0, nf)], o_sem.at[g])
        cp.start()
        copies.append(cp)

    for cp in copies:
        cp.wait()


def solution(mesh):
    n_tm, n_sp = mesh.shape["tm"], mesh.shape["space"]
    n = n_tm * n_sp

    def on_device(snapshots, basis, mass_table, elem_kind, offsets):
        rows, nvar, slab = snapshots.shape
        _, freqs, modes, _, pts = basis.shape
        blocks = offsets.shape[0]
        groups = -(-freqs // GROUP)
        entries = nvar * pts * n
        pairs = groups + -(-groups // 2)
        side = n_tm * n_sp
        upo = -(-pairs // side)
        owners = owner_list(n_tm, n_sp, -(-pairs // upo))
        table_rows = 2 * freqs * blocks
        unit = (2 * blocks, 2 * GROUP * blocks)
        chunks = tuple((v, min(v + 2, nvar)) for v in range(0, nvar, 2))
        snap = jnp.transpose(snapshots, (1, 0, 2))
        base = jnp.transpose(basis, (0, 1, 3, 2, 4))
        hbm = pl.BlockSpec(memory_space=pltpu.HBM)
        vmem = pl.BlockSpec(memory_space=pltpu.VMEM)
        spec, total = pl.pallas_call(
            functools.partial(kernel, n_tm, n_sp, owners, entries, chunks),
            out_shape=(
                jax.ShapeDtypeStruct((table_rows, nvar * pts), BF),
                jax.ShapeDtypeStruct((len(owners) * upo,) + unit, BF),
            ),
            in_specs=[hbm] * 5,
            out_specs=(vmem, vmem),
            scratch_shapes=[
                pltpu.VMEM((table_rows, rows * n_tm), BF),
                pltpu.VMEM((2, freqs, nvar, modes, pts), BF),
                pltpu.VMEM((len(owners) * upo,) + unit, BF),
                pltpu.VMEM((side, upo) + unit, BF),
                pltpu.VMEM((len(owners) * upo,) + unit, BF),
                pltpu.VMEM(mass_table.shape, F32),
                pltpu.SMEM(elem_kind.shape, jnp.int32),
                pltpu.SMEM(offsets.shape, jnp.int32),
            ]
            + [pltpu.VMEM((n_tm, v1 - v0, rows, pts), BF) for v0, v1 in chunks]
            + [
                pltpu.SemaphoreType.DMA((len(chunks),)),
                pltpu.SemaphoreType.DMA((len(chunks),)),
                pltpu.SemaphoreType.DMA((4,)),
                pltpu.SemaphoreType.REGULAR((3,)),
            ]
            + [pltpu.SemaphoreType.DMA] * 4,
            compiler_params=pltpu.CompilerParams(
                collective_id=0, has_side_effects=True, vmem_limit_bytes=48 * 1024 * 1024
            ),
        )(*[pltpu.with_memory_space_constraint(a, pltpu.HBM) for a in (snap, base, mass_table, elem_kind, offsets)])
        coef, new = pl.pallas_call(
            functools.partial(finish, entries),
            out_shape=(
                jax.ShapeDtypeStruct((2, blocks, modes, freqs), F32),
                jax.ShapeDtypeStruct(base.shape, BF),
            ),
            in_specs=[vmem, vmem],
            out_specs=(hbm, hbm),
            scratch_shapes=[
                pltpu.VMEM(base.shape, BF),
                pltpu.VMEM((2, blocks, modes, freqs), F32),
                pltpu.SemaphoreType.DMA((groups + 1,)),
            ],
            compiler_params=pltpu.CompilerParams(vmem_limit_bytes=32 * 1024 * 1024),
        )(total, spec)
        return jnp.transpose(coef, (0, 3, 1, 2)), jnp.transpose(new, (0, 1, 3, 2, 4))

    return jax.shard_map(
        on_device,
        mesh=mesh,
        in_specs=(
            P("tm", None, "space"),
            P(None, None, None, None, ("space", "tm")),
            P(),
            P(("space", "tm")),
            P(),
        ),
        out_specs=(P(), P(None, None, None, None, ("space", "tm"))),
        check_vma=False,
    )
```

```python
import functools
import math

import jax
import jax.numpy as jnp
from jax import lax
from jax.experimental import pallas as pl
from jax.experimental.pallas import tpu as pltpu
from jax.sharding import PartitionSpec as P

NT = 256
GROUP = 8
LEVELS = 4
MESH = pl.DeviceIdType.MESH
BF = jnp.bfloat16
F32 = jnp.float32


def owner_list(n_tm, n_sp, units):
    quart = n_tm // LEVELS
    chips = [(quart, 0), (quart + 2, 0), (quart, n_sp - 1)]
    spots = [(t + c, s) for t, s in chips for c in range(2)]
    each, extra = divmod(units, len(spots))
    sizes = [each + (i < extra) for i in range(len(spots))]
    return tuple((t, s, sum(sizes[:i]), sizes[i]) for i, (t, s) in enumerate(spots))


def tail_width(freqs, blocks, modes):
    width = 2 * (freqs % GROUP) * blocks
    return width if 0 < width * (1 + modes // blocks) <= 2 * GROUP * blocks else 0


def unit_count(freqs, blocks, modes):
    groups = -(-freqs // GROUP)
    per = 1 + modes // blocks
    return groups * per - (per - 1 if tail_width(freqs, blocks, modes) else 0)


def mm(a, b, contract):
    return lax.dot_general(a, b, (contract, ((), ())), preferred_element_type=F32)


def swap_halves(x, half):
    lanes = x.shape[1]
    if 2 * half == lanes:
        return pltpu.roll(x, half, 1)
    lane = lax.broadcasted_iota(jnp.int32, x.shape, 1)
    return jnp.where(lane < half, pltpu.roll(x, lanes - half, 1), pltpu.roll(x, half, 1))


def freq_mask(nf, rows, lanes, blocks):
    row_f = lax.broadcasted_iota(jnp.int32, (nf, rows, lanes), 0)
    lane = lax.broadcasted_iota(jnp.int32, (nf, rows, lanes), 2)
    half = nf * blocks
    return (row_f == lane % half // blocks) & (lane < 2 * half)


def kernel(
    n_tm, n_sp, owners, entries, chunks,
    snap, basis, mass_in, kinds_in, offs_in,
    sh, y_out,
    table, ub, xb, plane, yb, mass, kinds, offs, *rest,
):
    recs, (a_send, a_recv, l_sem, known, s1, r1, s2, r2) = rest[: len(chunks)], rest[len(chunks) :]
    tm = lax.axis_index("tm")
    sp = lax.axis_index("space")
    side = n_tm * n_sp
    scale = 1.0 / math.sqrt(entries)
    here = sp * n_tm + tm
    is_own = [(tm == t) & (sp == s) for t, s, _, _ in owners]
    quart = n_tm // LEVELS
    lev, place = lax.div(tm, quart), lax.rem(tm, quart)
    edge = (lev == 0) | (lev == LEVELS - 1)
    inward = jnp.where(lev < LEVELS // 2, 1, -1)
    freqs = basis.shape[1]
    rows, pts = recs[0].shape[2:]
    groups = -(-freqs // GROUP)
    counts = [min(GROUP, freqs - g * GROUP) for g in range(groups)]
    record = n_tm * rows
    blocks = offs.shape[0]
    modes = basis.shape[3]
    lanes = 2 * GROUP * blocks

    barrier = pltpu.get_barrier_semaphore()

    def signal(sem, to_tm, to_sp):
        pl.semaphore_signal(
            sem, inc=1, device_id={"tm": to_tm, "space": to_sp}, device_id_type=MESH
        )

    for dl in (1, -1, 0):

        def greet(i, carry):
            to = (lev + dl) * quart + lax.rem(place + i, quart)
            signal(barrier, to, sp)
            return carry

        @pl.when((lev + dl >= 0) & (lev + dl < LEVELS) & ((dl != -1) | (lev <= LEVELS // 2)))
        def _():
            lax.fori_loop(1 if dl == 0 else 0, quart, greet, 0, unroll=side <= 32)

    def greet_side(i, carry):
        signal(barrier, tm, lax.rem(sp + i, n_sp))
        return carry

    lax.fori_loop(1, n_sp, greet_side, 0, unroll=side <= 32)
    loads = [
        pltpu.make_async_copy(offs_in, offs, l_sem.at[0]),
        pltpu.make_async_copy(kinds_in, kinds, l_sem.at[1]),
        pltpu.make_async_copy(mass_in, mass, l_sem.at[2]),
        pltpu.make_async_copy(basis, ub, l_sem.at[3]),
    ]
    for cp in loads:
        cp.start()
    near = jnp.where((lev == 0) | (lev >= LEVELS // 2), 2, 3)
    pl.semaphore_wait(barrier, near * quart - 1 + n_sp - 1)

    def relay(stage, ways=(1, -1)):
        for dl in ways:
            seen = lev - dl * (stage - 1)

            @pl.when((seen >= 0) & (seen < LEVELS) & (lev + dl >= 0) & (lev + dl < LEVELS))
            def _():
                signal(known.at[stage - 2], tm + dl * quart, sp)

    def learn(stage):
        for dl in (1, -1):

            @pl.when((lev + dl * stage >= 0) & (lev + dl * stage < LEVELS))
            def _():
                pl.semaphore_wait(known.at[stage - 2], 1)

    def send_level(ci, to_lev, first=0):
        v0, v1 = chunks[ci]

        def send(i, carry):
            to = to_lev * quart + lax.rem(place + i, quart)
            pltpu.make_async_remote_copy(
                snap.at[pl.ds(v0, v1 - v0), :, pl.ds(pl.multiple_of(to * pts, pts), pts)],
                recs[ci].at[tm], a_send.at[ci], a_recv.at[ci],
                device_id={"tm": to, "space": sp}, device_id_type=MESH,
            ).start()
            return carry

        lax.fori_loop(first, quart, send, 0, unroll=side <= 32)

    turn = lev == LEVELS // 2
    pl.when(jnp.logical_not(turn))(lambda: relay(2))
    pl.when(lev > LEVELS // 2)(lambda: signal(known.at[3], tm - quart, sp))
    for ci, (v0, v1) in enumerate(chunks):
        mine = snap.at[pl.ds(v0, v1 - v0), :, pl.ds(pl.multiple_of(tm * pts, pts), pts)]
        if ci == 0:
            send_level(ci, lev + inward)
            pl.when(jnp.logical_not(edge | turn))(lambda: send_level(ci, lev - inward))
            send_level(ci, lev, 1)
            learn(2)
            pl.when(jnp.logical_not(turn))(lambda: relay(3))
            send_level(ci, lev + 2 * inward)

            @pl.when(turn)
            def _():
                pl.semaphore_wait(known.at[3], 1)
                relay(2)
                relay(3)
                send_level(ci, lev - inward)

            learn(3)
            pl.when(edge)(lambda: send_level(ci, lev + 3 * inward))

            def tell(i, carry):
                signal(known.at[2], tm, lax.rem(sp + i, n_sp))
                return carry

            lax.fori_loop(1, n_sp, tell, 0, unroll=side <= 32)
        else:
            pl.when(edge)(lambda: send_level(ci, lev + 3 * inward))
            send_level(ci, lev + 2 * inward)
            send_level(ci, lev + inward)
            pl.when(jnp.logical_not(edge))(lambda: send_level(ci, lev - inward))
            send_level(ci, lev, 1)
        pltpu.make_async_copy(mine, recs[ci].at[tm], a_recv.at[ci]).start()

    loads[0].wait()
    row = lax.broadcasted_iota(jnp.int32, (blocks, record), 0)
    lag = lax.broadcasted_iota(jnp.int32, (blocks, record), 1)
    for b in range(blocks):
        lag = jnp.where(row == b, lag - offs[b], lag)
    inside = (lag >= 0) & (lag < NT)
    theta = jnp.clip(lag, 0, NT - 1).astype(F32) * (2.0 * math.pi / NT)
    c1, s1v = jnp.cos(theta), jnp.sin(theta)
    win = jnp.where(inside, (0.5 - 0.5 * c1) * (1.0 / math.sqrt(0.375 * NT)), 0.0)
    cc, ss = win, jnp.zeros_like(win)
    for g, nf in enumerate(counts):
        parts = []
        for _ in range(nf):
            parts.append((cc, -ss))
            cc, ss = cc * c1 - ss * s1v, ss * c1 + cc * s1v
        table[g * lanes : g * lanes + 2 * nf * blocks] = jnp.concatenate(
            [p[c] for c in range(2) for p in parts], axis=0
        ).astype(BF)

    loads[1].wait()
    loads[2].wait()
    size = mass.shape[1]
    elems = pts // size
    strips = []
    for e in range(elems):
        kind = jnp.full((size, size), kinds[e], jnp.int32)
        blk = mass[0]
        for k in range(1, mass.shape[0]):
            blk = jnp.where(kind == k, mass[k], blk)
        zero = jnp.zeros_like(blk)
        strips.append(jnp.concatenate([blk if j == e else zero for j in range(elems)], axis=1))
    m_all = jnp.concatenate(strips, axis=0)
    m_hi = m_all.astype(BF)
    m_lo = (m_all - m_hi.astype(F32)).astype(BF)
    m_stack = jnp.concatenate([m_hi, m_hi, m_lo], axis=0)

    loads[3].wait()
    def fold(full, nf, rows):
        mask = freq_mask(nf, rows, lanes, blocks)
        real, imag = [
            jnp.sum(jnp.where(mask, part.reshape(nf, rows, lanes), 0.0), axis=0)
            for part in (full[: nf * rows], full[nf * rows :])
        ]
        imag = swap_halves(imag, nf * blocks)
        lane = lax.broadcasted_iota(jnp.int32, (rows, lanes), 1)
        return real + jnp.where(lane < nf * blocks, imag, -imag)

    coefs, grams = [None] * groups, [None] * groups
    for ci, (v0, v1) in enumerate(chunks):
        rec = recs[ci]
        pltpu.make_async_copy(rec, rec, a_recv.at[ci]).wait()
        count = v1 - v0
        x = jnp.concatenate([rec[:, v].reshape(record, pts) for v in range(count)], axis=1)
        cuts = [0, table.shape[0]] if count > 1 else [0, lanes * (groups // 2), table.shape[0]]
        spec = jnp.concatenate([mm(table[i:j], x, ((1,), (0,))) for i, j in zip(cuts, cuts[1:])], axis=0)
        s_hi = spec.astype(BF)
        s_lo = (spec - s_hi.astype(F32)).astype(BF)
        sh[:, v0 * pts : v1 * pts] = s_hi
        wts = []
        for v in range(count):
            cut = slice(v * pts, (v + 1) * pts)
            lhs = jnp.concatenate([s_hi[:, cut], s_lo[:, cut], s_hi[:, cut]], axis=1)
            wts.append(
                jnp.concatenate(
                    [mm(lhs[i:j], m_stack, ((1,), (0,))).astype(BF) for i, j in zip(cuts, cuts[1:])], axis=0
                )
            )
        wt = jnp.concatenate(wts, axis=1)
        for g, nf in enumerate(counts):
            cut = slice(g * lanes, g * lanes + 2 * nf * blocks)
            f0 = g * GROUP
            u = [
                jnp.concatenate(
                    [ub[c, f0 : f0 + nf, v].reshape(nf * modes, pts) for v in range(v0, v1)], axis=1
                )
                for c in range(2)
            ]
            w = wt[cut]
            if w.shape[0] < lanes:
                w = jnp.concatenate([w, jnp.zeros((lanes - w.shape[0], w.shape[1]), BF)], axis=0)
            full = mm(jnp.concatenate(u + [s_hi[cut]], axis=0), w, ((1,), (1,)))
            coef = fold(full[: 2 * nf * modes], nf, modes) * scale
            gram = fold(full[2 * nf * modes :], nf, blocks)
            coefs[g] = coef if ci == 0 else coefs[g] + coef
            grams[g] = gram if ci == 0 else grams[g] + gram
    width = tail_width(freqs, blocks, modes)
    per = modes // blocks
    tiles = [t for c in coefs for t in (c[i * blocks : (i + 1) * blocks] for i in range(per))]
    if width:
        lane = lax.broadcasted_iota(jnp.int32, (blocks, lanes), 1)
        tail = grams.pop()
        for i, t in enumerate(tiles[-per:]):
            tail = jnp.where(lane < (i + 1) * width, tail, pltpu.roll(t, (i + 1) * width, 1))
        tiles = tiles[:-per] + grams + [tail]
    else:
        tiles = tiles + grams
    for at, tile in enumerate(tiles):
        xb[at] = tile.astype(BF)

    pl.semaphore_wait(known.at[2], n_sp - 1)
    units = xb.shape[0]
    for t, s, first, size in owners:

        @pl.when((tm != t) | (sp != s))
        def _():
            pltpu.make_async_remote_copy(
                xb.at[pl.ds(first, size)], plane.at[here, pl.ds(0, size)], s1, r1,
                device_id={"tm": t, "space": s}, device_id_type=MESH,
            ).start()

    def wait_bytes(ref, sem):
        pltpu.make_async_copy(ref, ref, sem).wait()

    kinds_of = sorted({size for _, _, _, size in owners})
    holds = [
        (size, functools.reduce(jnp.logical_or, [m for m, o in zip(is_own, owners) if o[3] == size]))
        for size in kinds_of
    ]
    begin = sum(jnp.where(m, o[2], 0) for m, o in zip(is_own, owners))
    other = jnp.logical_not(functools.reduce(jnp.logical_or, is_own))
    for size, flag in holds:

        @pl.when(flag)
        def _():
            mine = pl.ds(begin, size)
            plane[here, 0:size] = xb[mine]
            wait_bytes(plane.at[pl.ds(0, side - 1), pl.ds(0, size)], r1)
            yb[mine] = jnp.sum(plane[:, 0:size].astype(F32), axis=0).astype(BF)

            def gather(i, carry):
                @pl.when(i != tm * n_sp + sp)
                def _():
                    pltpu.make_async_remote_copy(
                        yb.at[mine], yb.at[mine], s2, r2,
                        device_id={"tm": lax.div(i, n_sp), "space": lax.rem(i, n_sp)},
                        device_id_type=MESH,
                    ).start()

                return carry

            lax.fori_loop(0, side, gather, 0, unroll=side <= 32)
            wait_bytes(yb.at[pl.ds(0, units - size)], r2)

    @pl.when(other)
    def _():
        wait_bytes(yb, r2)

    y_out[...] = yb[...]
    for ci in range(len(chunks)):
        wait_bytes(recs[ci].at[pl.ds(0, n_tm - 1)], a_send.at[ci])
    for size, flag in holds:

        @pl.when(flag)
        def _():
            wait_bytes(xb.at[pl.ds(0, units - size)], s1)
            wait_bytes(plane.at[pl.ds(0, side - 1), pl.ds(0, size)], s2)

    @pl.when(other)
    def _():
        wait_bytes(xb, s1)


def finish(entries, yb, sh, coef_hbm, new_out, ob, coef_out, o_sem):
    freqs, nvar, modes, pts = new_out.shape[1:]
    blocks = coef_out.shape[1]
    lanes = yb.shape[2]
    groups = -(-freqs // GROUP)
    lane = lax.broadcasted_iota(jnp.int32, (modes, lanes), 1)
    lane_b = lane[:blocks]

    width = tail_width(freqs, blocks, modes)
    per = modes // blocks
    units = [yb[at].astype(F32) for at in range(yb.shape[0])]
    whole = groups - 1 if width else groups
    tiles = [jnp.concatenate(units[g * per : (g + 1) * per], axis=0) for g in range(whole)]
    grams = units[whole * per : whole * per + whole]
    if width:
        cuts = [pltpu.roll(units[-1], lanes - i * width, 1) if i else units[-1] for i in range(1 + per)]
        cuts = [jnp.where(lane_b < width, c, 0.0) for c in cuts]
        grams.append(cuts[0])
        tiles.append(jnp.concatenate(cuts[1:], axis=0))
    copies = []
    row_b = lax.broadcasted_iota(jnp.int32, (blocks, modes, lanes), 0)
    pick = row_b == lax.broadcasted_iota(jnp.int32, (blocks, modes, lanes), 2) % blocks
    picked = [
        jnp.where(pick, jnp.broadcast_to(t[None], pick.shape), 0.0).reshape(blocks * modes, lanes)
        for t in tiles
    ]
    lhs = jnp.concatenate(picked, axis=1).astype(BF)
    row = lax.broadcasted_iota(jnp.int32, (lanes, freqs), 0)
    col = lax.broadcasted_iota(jnp.int32, (lanes, freqs), 1)
    for c in range(2):
        moves = []
        for g in range(groups):
            half = min(GROUP, freqs - g * GROUP) * blocks
            hit = (row // half == c) & (col == row % half // blocks + g * GROUP)
            moves.append(jnp.where(hit, 1.0, 0.0).astype(BF))
        moved = mm(lhs, jnp.concatenate(moves, axis=0), ((1,), (0,)))
        coef_out[c] = moved.reshape(blocks, modes, freqs)
    cp = pltpu.make_async_copy(coef_out, coef_hbm, o_sem.at[groups])
    cp.start()
    copies.append(cp)

    for g in range(groups):
        f0 = g * GROUP
        nf = min(GROUP, freqs - f0)
        half = nf * blocks

        def spread(val):
            rows = val.shape[0]
            big = jnp.broadcast_to(val[None], (nf, rows, lanes))
            return jnp.where(freq_mask(nf, rows, lanes, blocks), big, 0.0).reshape(nf * rows, lanes)

        coef = tiles[g]
        gram = grams[g]
        vec = spread(jnp.where(lane < half, coef, -coef))
        turned = swap_halves(gram, half)
        quad = jnp.concatenate([spread(gram), spread(jnp.where(lane_b < half, -turned, turned))], axis=0)
        rows = [vec[:, : 2 * half].astype(BF), spread(swap_halves(coef, half))[:, : 2 * half].astype(BF)]
        energy = jnp.sum(vec * mm(rows[0], quad.astype(BF), ((1,), (0,))), axis=1, keepdims=True)
        factor = 1.0 / jnp.sqrt(energy / entries + 1e-06)
        both = jnp.concatenate(rows, axis=0)
        fields = mm(both, sh[g * lanes : g * lanes + 2 * half], ((1,), (0,)))
        for v in range(nvar):
            for c in range(2):
                val = (fields[c * nf * modes : (c + 1) * nf * modes, v * pts : (v + 1) * pts] * factor).astype(BF)
                ob[c, f0 : f0 + nf, v] = val.reshape(nf, modes, pts)
        cp = pltpu.make_async_copy(ob.at[:, pl.ds(f0, nf)], new_out.at[:, pl.ds(f0, nf)], o_sem.at[g])
        cp.start()
        copies.append(cp)

    for cp in copies:
        cp.wait()


def solution(mesh):
    n_tm, n_sp = mesh.shape["tm"], mesh.shape["space"]
    n = n_tm * n_sp

    def on_device(snapshots, basis, mass_table, elem_kind, offsets):
        rows, nvar, slab = snapshots.shape
        _, freqs, modes, _, pts = basis.shape
        blocks = offsets.shape[0]
        groups = -(-freqs // GROUP)
        entries = nvar * pts * n
        side = n_tm * n_sp
        units = unit_count(freqs, blocks, modes)
        owners = owner_list(n_tm, n_sp, units)
        table_rows = 2 * freqs * blocks
        unit = (blocks, 2 * GROUP * blocks)
        chunks = tuple((v, min(v + 2, nvar)) for v in range(0, nvar, 2))
        snap = jnp.transpose(snapshots, (1, 0, 2))
        base = jnp.transpose(basis, (0, 1, 3, 2, 4))
        hbm = pl.BlockSpec(memory_space=pltpu.HBM)
        vmem = pl.BlockSpec(memory_space=pltpu.VMEM)
        spec, total = pl.pallas_call(
            functools.partial(kernel, n_tm, n_sp, owners, entries, chunks),
            out_shape=(
                jax.ShapeDtypeStruct((table_rows, nvar * pts), BF),
                jax.ShapeDtypeStruct((units,) + unit, BF),
            ),
            in_specs=[hbm] * 5,
            out_specs=(vmem, vmem),
            scratch_shapes=[
                pltpu.VMEM((table_rows, rows * n_tm), BF),
                pltpu.VMEM((2, freqs, nvar, modes, pts), BF),
                pltpu.VMEM((units,) + unit, BF),
                pltpu.VMEM((side, max(o[3] for o in owners)) + unit, BF),
                pltpu.VMEM((units,) + unit, BF),
                pltpu.VMEM(mass_table.shape, F32),
                pltpu.SMEM(elem_kind.shape, jnp.int32),
                pltpu.SMEM(offsets.shape, jnp.int32),
            ]
            + [pltpu.VMEM((n_tm, v1 - v0, rows, pts), BF) for v0, v1 in chunks]
            + [
                pltpu.SemaphoreType.DMA((len(chunks),)),
                pltpu.SemaphoreType.DMA((len(chunks),)),
                pltpu.SemaphoreType.DMA((4,)),
                pltpu.SemaphoreType.REGULAR((4,)),
            ]
            + [pltpu.SemaphoreType.DMA] * 4,
            compiler_params=pltpu.CompilerParams(
                collective_id=0, has_side_effects=True, vmem_limit_bytes=48 * 1024 * 1024
            ),
        )(*[pltpu.with_memory_space_constraint(a, pltpu.HBM) for a in (snap, base, mass_table, elem_kind, offsets)])
        coef, new = pl.pallas_call(
            functools.partial(finish, entries),
            out_shape=(
                jax.ShapeDtypeStruct((2, blocks, modes, freqs), F32),
                jax.ShapeDtypeStruct(base.shape, BF),
            ),
            in_specs=[vmem, vmem],
            out_specs=(hbm, hbm),
            scratch_shapes=[
                pltpu.VMEM(base.shape, BF),
                pltpu.VMEM((2, blocks, modes, freqs), F32),
                pltpu.SemaphoreType.DMA((groups + 1,)),
            ],
            compiler_params=pltpu.CompilerParams(vmem_limit_bytes=32 * 1024 * 1024),
        )(total, spec)
        return jnp.transpose(coef, (0, 3, 1, 2)), jnp.transpose(new, (0, 1, 3, 2, 4))

    return jax.shard_map(
        on_device,
        mesh=mesh,
        in_specs=(
            P("tm", None, "space"),
            P(None, None, None, None, ("space", "tm")),
            P(),
            P(("space", "tm")),
            P(),
        ),
        out_specs=(P(), P(None, None, None, None, ("space", "tm"))),
        check_vma=False,
    )
```

```python
import functools
import math

import jax
import jax.numpy as jnp
from jax import lax
from jax.experimental import pallas as pl
from jax.experimental.pallas import tpu as pltpu
from jax.sharding import PartitionSpec as P

NT = 256
GROUP = 8
LEVELS = 4
MESH = pl.DeviceIdType.MESH
BF = jnp.bfloat16
F32 = jnp.float32


def owner_list(n_tm, n_sp, units):
    quart = n_tm // LEVELS
    chips = [(quart, 0), (quart + 2, 0), (quart, n_sp - 1)]
    spots = [(t + c, s) for t, s in chips for c in range(2)]
    each, extra = divmod(units, len(spots))
    sizes = [each + (i < extra) for i in range(len(spots))]
    return tuple((t, s, sum(sizes[:i]), sizes[i]) for i, (t, s) in enumerate(spots))


def tail_width(freqs, blocks, modes):
    width = 2 * (freqs % GROUP) * blocks
    return width if 0 < width * (1 + modes // blocks) <= 2 * GROUP * blocks else 0


def unit_count(freqs, blocks, modes):
    groups = -(-freqs // GROUP)
    per = 1 + modes // blocks
    return groups * per - (per - 1 if tail_width(freqs, blocks, modes) else 0)


def mm(a, b, contract):
    return lax.dot_general(a, b, (contract, ((), ())), preferred_element_type=F32)


def swap_halves(x, half):
    lanes = x.shape[1]
    if 2 * half == lanes:
        return pltpu.roll(x, half, 1)
    lane = lax.broadcasted_iota(jnp.int32, x.shape, 1)
    return jnp.where(lane < half, pltpu.roll(x, lanes - half, 1), pltpu.roll(x, half, 1))


def freq_mask(nf, rows, lanes, blocks):
    row_f = lax.broadcasted_iota(jnp.int32, (nf, rows, lanes), 0)
    lane = lax.broadcasted_iota(jnp.int32, (nf, rows, lanes), 2)
    half = nf * blocks
    return (row_f == lane % half // blocks) & (lane < 2 * half)


def kernel(
    n_tm, n_sp, owners, entries, chunks,
    snap, basis, mass_in, kinds_in, offs_in,
    sh, y_out,
    table, ub, xb, plane, yb, mass, kinds, offs, *rest,
):
    recs, (a_send, a_recv, l_sem, known, s1, r1, s2, r2) = rest[: len(chunks)], rest[len(chunks) :]
    tm = lax.axis_index("tm")
    sp = lax.axis_index("space")
    side = n_tm * n_sp
    scale = 1.0 / math.sqrt(entries)
    here = sp * n_tm + tm
    is_own = [(tm == t) & (sp == s) for t, s, _, _ in owners]
    quart = n_tm // LEVELS
    lev, place = lax.div(tm, quart), lax.rem(tm, quart)
    edge = (lev == 0) | (lev == LEVELS - 1)
    inward = jnp.where(lev < LEVELS // 2, 1, -1)
    freqs = basis.shape[1]
    rows, pts = recs[0].shape[2:]
    groups = -(-freqs // GROUP)
    counts = [min(GROUP, freqs - g * GROUP) for g in range(groups)]
    record = n_tm * rows
    blocks = offs.shape[0]
    modes = basis.shape[3]
    lanes = 2 * GROUP * blocks

    barrier = pltpu.get_barrier_semaphore()

    def signal(sem, to_tm, to_sp):
        pl.semaphore_signal(
            sem, inc=1, device_id={"tm": to_tm, "space": to_sp}, device_id_type=MESH
        )

    for dl in (1, -1, 0):

        def greet(i, carry):
            to = (lev + dl) * quart + lax.rem(place + i, quart)
            signal(barrier, to, sp)
            return carry

        @pl.when((lev + dl >= 0) & (lev + dl < LEVELS) & ((dl != -1) | (lev <= LEVELS // 2)))
        def _():
            lax.fori_loop(1 if dl == 0 else 0, quart, greet, 0, unroll=side <= 32)

    def greet_side(i, carry):
        signal(barrier, tm, lax.rem(sp + i, n_sp))
        return carry

    lax.fori_loop(1, n_sp, greet_side, 0, unroll=side <= 32)
    loads = [
        pltpu.make_async_copy(offs_in, offs, l_sem.at[0]),
        pltpu.make_async_copy(kinds_in, kinds, l_sem.at[1]),
        pltpu.make_async_copy(mass_in, mass, l_sem.at[2]),
        pltpu.make_async_copy(basis, ub, l_sem.at[3]),
    ]
    for cp in loads:
        cp.start()
    near = jnp.where((lev == 0) | (lev >= LEVELS // 2), 2, 3)
    pl.semaphore_wait(barrier, near * quart - 1 + n_sp - 1)

    def relay(stage, ways=(1, -1)):
        for dl in ways:
            seen = lev - dl * (stage - 1)

            @pl.when((seen >= 0) & (seen < LEVELS) & (lev + dl >= 0) & (lev + dl < LEVELS))
            def _():
                signal(known.at[stage - 2], tm + dl * quart, sp)

    def learn(stage):
        for dl in (1, -1):

            @pl.when((lev + dl * stage >= 0) & (lev + dl * stage < LEVELS))
            def _():
                pl.semaphore_wait(known.at[stage - 2], 1)

    def send_level(ci, to_lev, first=0):
        v0, v1 = chunks[ci]

        def send(i, carry):
            to = to_lev * quart + (lax.rem(place + i, quart) if first else quart - 1 - i)
            pltpu.make_async_remote_copy(
                snap.at[pl.ds(v0, v1 - v0), :, pl.ds(pl.multiple_of(to * pts, pts), pts)],
                recs[ci].at[tm], a_send.at[ci], a_recv.at[ci],
                device_id={"tm": to, "space": sp}, device_id_type=MESH,
            ).start()
            return carry

        lax.fori_loop(first, quart, send, 0, unroll=side <= 32)

    turn = lev == LEVELS // 2
    pl.when(jnp.logical_not(turn))(lambda: relay(2))
    pl.when(lev > LEVELS // 2)(lambda: signal(known.at[3], tm - quart, sp))
    for ci, (v0, v1) in enumerate(chunks):
        mine = snap.at[pl.ds(v0, v1 - v0), :, pl.ds(pl.multiple_of(tm * pts, pts), pts)]
        if ci == 0:
            send_level(ci, lev + inward)
            pl.when(jnp.logical_not(edge | turn))(lambda: send_level(ci, lev - inward))
            send_level(ci, lev, 1)
            learn(2)
            pl.when(jnp.logical_not(turn))(lambda: relay(3))
            send_level(ci, lev + 2 * inward)

            @pl.when(turn)
            def _():
                pl.semaphore_wait(known.at[3], 1)
                relay(2)
                relay(3)
                send_level(ci, lev - inward)

            learn(3)
            pl.when(edge)(lambda: send_level(ci, lev + 3 * inward))

            def tell(i, carry):
                signal(known.at[2], tm, lax.rem(sp + i, n_sp))
                return carry

            lax.fori_loop(1, n_sp, tell, 0, unroll=side <= 32)
        else:
            pl.when(edge)(lambda: send_level(ci, lev + 3 * inward))
            send_level(ci, lev + 2 * inward)
            send_level(ci, lev + inward)
            pl.when(jnp.logical_not(edge))(lambda: send_level(ci, lev - inward))
            send_level(ci, lev, 1)
        pltpu.make_async_copy(mine, recs[ci].at[tm], a_recv.at[ci]).start()

    loads[0].wait()
    row = lax.broadcasted_iota(jnp.int32, (blocks, record), 0)
    lag = lax.broadcasted_iota(jnp.int32, (blocks, record), 1)
    for b in range(blocks):
        lag = jnp.where(row == b, lag - offs[b], lag)
    inside = (lag >= 0) & (lag < NT)
    theta = jnp.clip(lag, 0, NT - 1).astype(F32) * (2.0 * math.pi / NT)
    c1, s1v = jnp.cos(theta), jnp.sin(theta)
    win = jnp.where(inside, (0.5 - 0.5 * c1) * (1.0 / math.sqrt(0.375 * NT)), 0.0)
    cc, ss = win, jnp.zeros_like(win)
    for g, nf in enumerate(counts):
        parts = []
        for _ in range(nf):
            parts.append((cc, -ss))
            cc, ss = cc * c1 - ss * s1v, ss * c1 + cc * s1v
        table[g * lanes : g * lanes + 2 * nf * blocks] = jnp.concatenate(
            [p[c] for c in range(2) for p in parts], axis=0
        ).astype(BF)

    loads[1].wait()
    loads[2].wait()
    size = mass.shape[1]
    elems = pts // size
    strips = []
    for e in range(elems):
        kind = jnp.full((size, size), kinds[e], jnp.int32)
        blk = mass[0]
        for k in range(1, mass.shape[0]):
            blk = jnp.where(kind == k, mass[k], blk)
        zero = jnp.zeros_like(blk)
        strips.append(jnp.concatenate([blk if j == e else zero for j in range(elems)], axis=1))
    m_all = jnp.concatenate(strips, axis=0)
    m_hi = m_all.astype(BF)
    m_lo = (m_all - m_hi.astype(F32)).astype(BF)
    m_stack = jnp.concatenate([m_hi, m_hi, m_lo], axis=0)

    loads[3].wait()
    def fold(full, nf, rows):
        mask = freq_mask(nf, rows, lanes, blocks)
        real, imag = [
            jnp.sum(jnp.where(mask, part.reshape(nf, rows, lanes), 0.0), axis=0)
            for part in (full[: nf * rows], full[nf * rows :])
        ]
        imag = swap_halves(imag, nf * blocks)
        lane = lax.broadcasted_iota(jnp.int32, (rows, lanes), 1)
        return real + jnp.where(lane < nf * blocks, imag, -imag)

    coefs, grams = [None] * groups, [None] * groups
    for ci, (v0, v1) in enumerate(chunks):
        rec = recs[ci]
        pltpu.make_async_copy(rec, rec, a_recv.at[ci]).wait()
        count = v1 - v0
        x = jnp.concatenate([rec[:, v].reshape(record, pts) for v in range(count)], axis=1)
        cuts = [0, table.shape[0]] if count > 1 else [0, lanes, 2 * lanes, 3 * lanes, table.shape[0]]
        spec = jnp.concatenate([mm(table[i:j], x, ((1,), (0,))) for i, j in zip(cuts, cuts[1:])], axis=0)
        s_hi = spec.astype(BF)
        s_lo = (spec - s_hi.astype(F32)).astype(BF)
        sh[:, v0 * pts : v1 * pts] = s_hi
        wts = []
        for v in range(count):
            cut = slice(v * pts, (v + 1) * pts)
            lhs = jnp.concatenate([s_hi[:, cut], s_lo[:, cut], s_hi[:, cut]], axis=1)
            wts.append(
                jnp.concatenate(
                    [mm(lhs[i:j], m_stack, ((1,), (0,))).astype(BF) for i, j in zip(cuts, cuts[1:])], axis=0
                )
            )
        wt = jnp.concatenate(wts, axis=1)
        for g, nf in enumerate(counts):
            cut = slice(g * lanes, g * lanes + 2 * nf * blocks)
            f0 = g * GROUP
            u = [
                jnp.concatenate(
                    [ub[c, f0 : f0 + nf, v].reshape(nf * modes, pts) for v in range(v0, v1)], axis=1
                )
                for c in range(2)
            ]
            w = wt[cut]
            if w.shape[0] < lanes:
                w = jnp.concatenate([w, jnp.zeros((lanes - w.shape[0], w.shape[1]), BF)], axis=0)
            full = mm(jnp.concatenate(u + [s_hi[cut]], axis=0), w, ((1,), (1,)))
            coef = fold(full[: 2 * nf * modes], nf, modes) * scale
            gram = fold(full[2 * nf * modes :], nf, blocks)
            coefs[g] = coef if ci == 0 else coefs[g] + coef
            grams[g] = gram if ci == 0 else grams[g] + gram
    width = tail_width(freqs, blocks, modes)
    per = modes // blocks
    tiles = [t for c in coefs for t in (c[i * blocks : (i + 1) * blocks] for i in range(per))]
    if width:
        lane = lax.broadcasted_iota(jnp.int32, (blocks, lanes), 1)
        tail = grams.pop()
        for i, t in enumerate(tiles[-per:]):
            tail = jnp.where(lane < (i + 1) * width, tail, pltpu.roll(t, (i + 1) * width, 1))
        tiles = tiles[:-per] + grams + [tail]
    else:
        tiles = tiles + grams
    for at, tile in enumerate(tiles):
        xb[at] = tile.astype(BF)

    pl.semaphore_wait(known.at[2], n_sp - 1)
    units = xb.shape[0]
    for t, s, first, size in owners:

        @pl.when((tm != t) | (sp != s))
        def _():
            pltpu.make_async_remote_copy(
                xb.at[pl.ds(first, size)], plane.at[here, pl.ds(0, size)], s1, r1,
                device_id={"tm": t, "space": s}, device_id_type=MESH,
            ).start()

    def wait_bytes(ref, sem):
        pltpu.make_async_copy(ref, ref, sem).wait()

    kinds_of = sorted({size for _, _, _, size in owners})
    holds = [
        (size, functools.reduce(jnp.logical_or, [m for m, o in zip(is_own, owners) if o[3] == size]))
        for size in kinds_of
    ]
    begin = sum(jnp.where(m, o[2], 0) for m, o in zip(is_own, owners))
    other = jnp.logical_not(functools.reduce(jnp.logical_or, is_own))
    for size, flag in holds:

        @pl.when(flag)
        def _():
            mine = pl.ds(begin, size)
            plane[here, 0:size] = xb[mine]
            wait_bytes(plane.at[pl.ds(0, side - 1), pl.ds(0, size)], r1)
            yb[mine] = jnp.sum(plane[:, 0:size].astype(F32), axis=0).astype(BF)

            def gather(i, carry):
                @pl.when(i != tm * n_sp + sp)
                def _():
                    pltpu.make_async_remote_copy(
                        yb.at[mine], yb.at[mine], s2, r2,
                        device_id={"tm": lax.div(i, n_sp), "space": lax.rem(i, n_sp)},
                        device_id_type=MESH,
                    ).start()

                return carry

            lax.fori_loop(0, side, gather, 0, unroll=side <= 32)
            wait_bytes(yb.at[pl.ds(0, units - size)], r2)

    @pl.when(other)
    def _():
        wait_bytes(yb, r2)

    y_out[...] = yb[...]
    for ci in range(len(chunks)):
        wait_bytes(recs[ci].at[pl.ds(0, n_tm - 1)], a_send.at[ci])
    for size, flag in holds:

        @pl.when(flag)
        def _():
            wait_bytes(xb.at[pl.ds(0, units - size)], s1)
            wait_bytes(plane.at[pl.ds(0, side - 1), pl.ds(0, size)], s2)

    @pl.when(other)
    def _():
        wait_bytes(xb, s1)


def finish(entries, yb, sh, coef_hbm, new_out, ob, coef_out, o_sem):
    freqs, nvar, modes, pts = new_out.shape[1:]
    blocks = coef_out.shape[1]
    lanes = yb.shape[2]
    groups = -(-freqs // GROUP)
    lane = lax.broadcasted_iota(jnp.int32, (modes, lanes), 1)
    lane_b = lane[:blocks]

    width = tail_width(freqs, blocks, modes)
    per = modes // blocks
    units = [yb[at].astype(F32) for at in range(yb.shape[0])]
    whole = groups - 1 if width else groups
    tiles = [jnp.concatenate(units[g * per : (g + 1) * per], axis=0) for g in range(whole)]
    grams = units[whole * per : whole * per + whole]
    if width:
        cuts = [pltpu.roll(units[-1], lanes - i * width, 1) if i else units[-1] for i in range(1 + per)]
        cuts = [jnp.where(lane_b < width, c, 0.0) for c in cuts]
        grams.append(cuts[0])
        tiles.append(jnp.concatenate(cuts[1:], axis=0))
    copies = []
    row_b = lax.broadcasted_iota(jnp.int32, (blocks, modes, lanes), 0)
    pick = row_b == lax.broadcasted_iota(jnp.int32, (blocks, modes, lanes), 2) % blocks
    picked = [
        jnp.where(pick, jnp.broadcast_to(t[None], pick.shape), 0.0).reshape(blocks * modes, lanes)
        for t in tiles
    ]
    lhs = jnp.concatenate(picked, axis=1).astype(BF)
    row = lax.broadcasted_iota(jnp.int32, (lanes, freqs), 0)
    col = lax.broadcasted_iota(jnp.int32, (lanes, freqs), 1)
    for c in range(2):
        moves = []
        for g in range(groups):
            half = min(GROUP, freqs - g * GROUP) * blocks
            hit = (row // half == c) & (col == row % half // blocks + g * GROUP)
            moves.append(jnp.where(hit, 1.0, 0.0).astype(BF))
        moved = mm(lhs, jnp.concatenate(moves, axis=0), ((1,), (0,)))
        coef_out[c] = moved.reshape(blocks, modes, freqs)
    cp = pltpu.make_async_copy(coef_out, coef_hbm, o_sem.at[groups])
    cp.start()
    copies.append(cp)

    for g in range(groups):
        f0 = g * GROUP
        nf = min(GROUP, freqs - f0)
        half = nf * blocks

        def spread(val):
            rows = val.shape[0]
            big = jnp.broadcast_to(val[None], (nf, rows, lanes))
            return jnp.where(freq_mask(nf, rows, lanes, blocks), big, 0.0).reshape(nf * rows, lanes)

        coef = tiles[g]
        gram = grams[g]
        vec = spread(jnp.where(lane < half, coef, -coef))
        turned = swap_halves(gram, half)
        quad = jnp.concatenate([spread(gram), spread(jnp.where(lane_b < half, -turned, turned))], axis=0)
        rows = [vec[:, : 2 * half].astype(BF), spread(swap_halves(coef, half))[:, : 2 * half].astype(BF)]
        energy = jnp.sum(vec * mm(rows[0], quad.astype(BF), ((1,), (0,))), axis=1, keepdims=True)
        factor = 1.0 / jnp.sqrt(energy / entries + 1e-06)
        both = jnp.concatenate(rows, axis=0)
        fields = mm(both, sh[g * lanes : g * lanes + 2 * half], ((1,), (0,)))
        for v in range(nvar):
            for c in range(2):
                val = (fields[c * nf * modes : (c + 1) * nf * modes, v * pts : (v + 1) * pts] * factor).astype(BF)
                ob[c, f0 : f0 + nf, v] = val.reshape(nf, modes, pts)
        cp = pltpu.make_async_copy(ob.at[:, pl.ds(f0, nf)], new_out.at[:, pl.ds(f0, nf)], o_sem.at[g])
        cp.start()
        copies.append(cp)

    for cp in copies:
        cp.wait()


def solution(mesh):
    n_tm, n_sp = mesh.shape["tm"], mesh.shape["space"]
    n = n_tm * n_sp

    def on_device(snapshots, basis, mass_table, elem_kind, offsets):
        rows, nvar, slab = snapshots.shape
        _, freqs, modes, _, pts = basis.shape
        blocks = offsets.shape[0]
        groups = -(-freqs // GROUP)
        entries = nvar * pts * n
        side = n_tm * n_sp
        units = unit_count(freqs, blocks, modes)
        owners = owner_list(n_tm, n_sp, units)
        table_rows = 2 * freqs * blocks
        unit = (blocks, 2 * GROUP * blocks)
        chunks = tuple((v, min(v + 2, nvar)) for v in range(0, nvar, 2))
        snap = jnp.transpose(snapshots, (1, 0, 2))
        base = jnp.transpose(basis, (0, 1, 3, 2, 4))
        hbm = pl.BlockSpec(memory_space=pltpu.HBM)
        vmem = pl.BlockSpec(memory_space=pltpu.VMEM)
        spec, total = pl.pallas_call(
            functools.partial(kernel, n_tm, n_sp, owners, entries, chunks),
            out_shape=(
                jax.ShapeDtypeStruct((table_rows, nvar * pts), BF),
                jax.ShapeDtypeStruct((units,) + unit, BF),
            ),
            in_specs=[hbm] * 5,
            out_specs=(vmem, vmem),
            scratch_shapes=[
                pltpu.VMEM((table_rows, rows * n_tm), BF),
                pltpu.VMEM((2, freqs, nvar, modes, pts), BF),
                pltpu.VMEM((units,) + unit, BF),
                pltpu.VMEM((side, max(o[3] for o in owners)) + unit, BF),
                pltpu.VMEM((units,) + unit, BF),
                pltpu.VMEM(mass_table.shape, F32),
                pltpu.SMEM(elem_kind.shape, jnp.int32),
                pltpu.SMEM(offsets.shape, jnp.int32),
            ]
            + [pltpu.VMEM((n_tm, v1 - v0, rows, pts), BF) for v0, v1 in chunks]
            + [
                pltpu.SemaphoreType.DMA((len(chunks),)),
                pltpu.SemaphoreType.DMA((len(chunks),)),
                pltpu.SemaphoreType.DMA((4,)),
                pltpu.SemaphoreType.REGULAR((4,)),
            ]
            + [pltpu.SemaphoreType.DMA] * 4,
            compiler_params=pltpu.CompilerParams(
                collective_id=0, has_side_effects=True, vmem_limit_bytes=48 * 1024 * 1024
            ),
        )(*[pltpu.with_memory_space_constraint(a, pltpu.HBM) for a in (snap, base, mass_table, elem_kind, offsets)])
        coef, new = pl.pallas_call(
            functools.partial(finish, entries),
            out_shape=(
                jax.ShapeDtypeStruct((2, blocks, modes, freqs), F32),
                jax.ShapeDtypeStruct(base.shape, BF),
            ),
            in_specs=[vmem, vmem],
            out_specs=(hbm, hbm),
            scratch_shapes=[
                pltpu.VMEM(base.shape, BF),
                pltpu.VMEM((2, blocks, modes, freqs), F32),
                pltpu.SemaphoreType.DMA((groups + 1,)),
            ],
            compiler_params=pltpu.CompilerParams(vmem_limit_bytes=32 * 1024 * 1024),
        )(total, spec)
        return jnp.transpose(coef, (0, 3, 1, 2)), jnp.transpose(new, (0, 1, 3, 2, 4))

    return jax.shard_map(
        on_device,
        mesh=mesh,
        in_specs=(
            P("tm", None, "space"),
            P(None, None, None, None, ("space", "tm")),
            P(),
            P(("space", "tm")),
            P(),
        ),
        out_specs=(P(), P(None, None, None, None, ("space", "tm"))),
        check_vma=False,
    )
```

```python
import functools
import math

import jax
import jax.numpy as jnp
from jax import lax
from jax.experimental import pallas as pl
from jax.experimental.pallas import tpu as pltpu
from jax.sharding import PartitionSpec as P

NT = 256
GROUP = 8
LEVELS = 4
MESH = pl.DeviceIdType.MESH
BF = jnp.bfloat16
F32 = jnp.float32


def owner_list(n_tm, n_sp, units):
    quart = n_tm // LEVELS
    chips = [(quart, 0), (quart + 2, 0), (quart, n_sp - 1)]
    spots = [(t + c, s) for t, s in chips for c in range(2)]
    each, extra = divmod(units, len(spots))
    sizes = [each + (i < extra) for i in range(len(spots))]
    return tuple((t, s, sum(sizes[:i]), sizes[i]) for i, (t, s) in enumerate(spots))


def tail_width(freqs, blocks, modes):
    width = 2 * (freqs % GROUP) * blocks
    return width if 0 < width * (1 + modes // blocks) <= 2 * GROUP * blocks else 0


def unit_count(freqs, blocks, modes):
    groups = -(-freqs // GROUP)
    per = 1 + modes // blocks
    return groups * per - (per - 1 if tail_width(freqs, blocks, modes) else 0)


def mm(a, b, contract):
    return lax.dot_general(a, b, (contract, ((), ())), preferred_element_type=F32)


def swap_halves(x, half):
    lanes = x.shape[1]
    if 2 * half == lanes:
        return pltpu.roll(x, half, 1)
    lane = lax.broadcasted_iota(jnp.int32, x.shape, 1)
    return jnp.where(lane < half, pltpu.roll(x, lanes - half, 1), pltpu.roll(x, half, 1))


def freq_mask(nf, rows, lanes, blocks):
    row_f = lax.broadcasted_iota(jnp.int32, (nf, rows, lanes), 0)
    lane = lax.broadcasted_iota(jnp.int32, (nf, rows, lanes), 2)
    half = nf * blocks
    return (row_f == lane % half // blocks) & (lane < 2 * half)


def kernel(
    n_tm, n_sp, owners, entries, chunks,
    snap, basis, mass_in, kinds_in, offs_in,
    sh, y_out,
    table, ub, xb, plane, yb, mass, kinds, offs, *rest,
):
    recs, (a_send, a_recv, l_sem, known, s1, r1, s2, r2) = rest[: len(chunks)], rest[len(chunks) :]
    tm = lax.axis_index("tm")
    sp = lax.axis_index("space")
    side = n_tm * n_sp
    scale = 1.0 / math.sqrt(entries)
    here = sp * n_tm + tm
    is_own = [(tm == t) & (sp == s) for t, s, _, _ in owners]
    quart = n_tm // LEVELS
    lev, place = lax.div(tm, quart), lax.rem(tm, quart)
    edge = (lev == 0) | (lev == LEVELS - 1)
    inward = jnp.where(lev < LEVELS // 2, 1, -1)
    freqs = basis.shape[1]
    rows, pts = recs[0].shape[2:]
    groups = -(-freqs // GROUP)
    counts = [min(GROUP, freqs - g * GROUP) for g in range(groups)]
    record = n_tm * rows
    blocks = offs.shape[0]
    modes = basis.shape[3]
    lanes = 2 * GROUP * blocks

    barrier = pltpu.get_barrier_semaphore()

    def signal(sem, to_tm, to_sp):
        pl.semaphore_signal(
            sem, inc=1, device_id={"tm": to_tm, "space": to_sp}, device_id_type=MESH
        )

    for dl in (1, -1, 0):

        def greet(i, carry):
            to = (lev + dl) * quart + lax.rem(place + i, quart)
            signal(barrier, to, sp)
            return carry

        @pl.when((lev + dl >= 0) & (lev + dl < LEVELS) & ((dl != -1) | (lev <= LEVELS // 2)))
        def _():
            lax.fori_loop(1 if dl == 0 else 0, quart, greet, 0, unroll=side <= 32)

    def greet_side(i, carry):
        signal(barrier, tm, lax.rem(sp + i, n_sp))
        return carry

    lax.fori_loop(1, n_sp, greet_side, 0, unroll=side <= 32)
    loads = [
        pltpu.make_async_copy(offs_in, offs, l_sem.at[0]),
        pltpu.make_async_copy(kinds_in, kinds, l_sem.at[1]),
        pltpu.make_async_copy(mass_in, mass, l_sem.at[2]),
        pltpu.make_async_copy(basis, ub, l_sem.at[3]),
    ]
    for cp in loads:
        cp.start()
    near = jnp.where((lev == 0) | (lev >= LEVELS // 2), 2, 3)
    pl.semaphore_wait(barrier, near * quart - 1 + n_sp - 1)

    def relay(stage, ways=(1, -1)):
        for dl in ways:
            seen = lev - dl * (stage - 1)

            @pl.when((seen >= 0) & (seen < LEVELS) & (lev + dl >= 0) & (lev + dl < LEVELS))
            def _():
                signal(known.at[stage - 2], tm + dl * quart, sp)

    def learn(stage):
        for dl in (1, -1):

            @pl.when((lev + dl * stage >= 0) & (lev + dl * stage < LEVELS))
            def _():
                pl.semaphore_wait(known.at[stage - 2], 1)

    def send_level(ci, to_lev, first=0):
        v0, v1 = chunks[ci]

        def send(i, carry):
            to = to_lev * quart + (lax.rem(place + i, quart) if first else quart - 1 - i)
            pltpu.make_async_remote_copy(
                snap.at[pl.ds(v0, v1 - v0), :, pl.ds(pl.multiple_of(to * pts, pts), pts)],
                recs[ci].at[tm], a_send.at[ci], a_recv.at[ci],
                device_id={"tm": to, "space": sp}, device_id_type=MESH,
            ).start()
            return carry

        lax.fori_loop(first, quart, send, 0, unroll=side <= 32)

    turn = lev == LEVELS // 2
    pl.when(jnp.logical_not(turn))(lambda: relay(2))
    pl.when(lev > LEVELS // 2)(lambda: signal(known.at[3], tm - quart, sp))
    for ci, (v0, v1) in enumerate(chunks):
        mine = snap.at[pl.ds(v0, v1 - v0), :, pl.ds(pl.multiple_of(tm * pts, pts), pts)]
        if ci == 0:
            send_level(ci, lev + inward)
            pl.when(jnp.logical_not(edge | turn))(lambda: send_level(ci, lev - inward))
            send_level(ci, lev, 1)
            learn(2)
            pl.when(jnp.logical_not(turn))(lambda: relay(3))
            send_level(ci, lev + 2 * inward)

            @pl.when(turn)
            def _():
                pl.semaphore_wait(known.at[3], 1)
                relay(2)
                relay(3)
                send_level(ci, lev - inward)

            learn(3)
            pl.when(edge)(lambda: send_level(ci, lev + 3 * inward))

            def tell(i, carry):
                signal(known.at[2], tm, lax.rem(sp + i, n_sp))
                return carry

            lax.fori_loop(1, n_sp, tell, 0, unroll=side <= 32)
        else:
            pl.when(edge)(lambda: send_level(ci, lev + 3 * inward))
            send_level(ci, lev + 2 * inward)
            send_level(ci, lev + inward)
            pl.when(jnp.logical_not(edge))(lambda: send_level(ci, lev - inward))
            send_level(ci, lev, 1)
        pltpu.make_async_copy(mine, recs[ci].at[tm], a_recv.at[ci]).start()

    loads[0].wait()
    row = lax.broadcasted_iota(jnp.int32, (blocks, record), 0)
    lag = lax.broadcasted_iota(jnp.int32, (blocks, record), 1)
    for b in range(blocks):
        lag = jnp.where(row == b, lag - offs[b], lag)
    inside = (lag >= 0) & (lag < NT)
    theta = jnp.clip(lag, 0, NT - 1).astype(F32) * (2.0 * math.pi / NT)
    c1, s1v = jnp.cos(theta), jnp.sin(theta)
    win = jnp.where(inside, (0.5 - 0.5 * c1) * (1.0 / math.sqrt(0.375 * NT)), 0.0)
    cc, ss = win, jnp.zeros_like(win)
    for g, nf in enumerate(counts):
        parts = []
        for _ in range(nf):
            parts.append((cc, -ss))
            cc, ss = cc * c1 - ss * s1v, ss * c1 + cc * s1v
        table[g * lanes : g * lanes + 2 * nf * blocks] = jnp.concatenate(
            [p[c] for c in range(2) for p in parts], axis=0
        ).astype(BF)

    loads[1].wait()
    loads[2].wait()
    size = mass.shape[1]
    elems = pts // size
    strips = []
    for e in range(elems):
        kind = jnp.full((size, size), kinds[e], jnp.int32)
        blk = mass[0]
        for k in range(1, mass.shape[0]):
            blk = jnp.where(kind == k, mass[k], blk)
        zero = jnp.zeros_like(blk)
        strips.append(jnp.concatenate([blk if j == e else zero for j in range(elems)], axis=1))
    m_all = jnp.concatenate(strips, axis=0)
    m_hi = m_all.astype(BF)
    m_lo = (m_all - m_hi.astype(F32)).astype(BF)
    m_stack = jnp.concatenate([m_hi, m_hi, m_lo], axis=0)

    loads[3].wait()
    def fold(full, nf, rows):
        mask = freq_mask(nf, rows, lanes, blocks)
        real, imag = [
            jnp.sum(jnp.where(mask, part.reshape(nf, rows, lanes), 0.0), axis=0)
            for part in (full[: nf * rows], full[nf * rows :])
        ]
        imag = swap_halves(imag, nf * blocks)
        lane = lax.broadcasted_iota(jnp.int32, (rows, lanes), 1)
        return real + jnp.where(lane < nf * blocks, imag, -imag)

    coefs, grams = [None] * groups, [None] * groups
    for ci, (v0, v1) in enumerate(chunks):
        rec = recs[ci]
        pltpu.make_async_copy(rec, rec, a_recv.at[ci]).wait()
        count = v1 - v0
        x = jnp.concatenate([rec[:, v].reshape(record, pts) for v in range(count)], axis=1)
        cuts = [0, table.shape[0]] if count > 1 else [0, lanes, 2 * lanes, 3 * lanes, table.shape[0]]
        spec = jnp.concatenate([mm(table[i:j], x, ((1,), (0,))) for i, j in zip(cuts, cuts[1:])], axis=0)
        s_hi = spec.astype(BF)
        s_lo = (spec - s_hi.astype(F32)).astype(BF)
        sh[:, v0 * pts : v1 * pts] = s_hi
        wts = []
        for v in range(count):
            cut = slice(v * pts, (v + 1) * pts)
            lhs = jnp.concatenate([s_hi[:, cut], s_lo[:, cut], s_hi[:, cut]], axis=1)
            wts.append(
                jnp.concatenate(
                    [mm(lhs[i:j], m_stack, ((1,), (0,))).astype(BF) for i, j in zip(cuts, cuts[1:])], axis=0
                )
            )
        wt = jnp.concatenate(wts, axis=1)
        for g, nf in enumerate(counts):
            cut = slice(g * lanes, g * lanes + 2 * nf * blocks)
            f0 = g * GROUP
            u = [
                jnp.concatenate(
                    [ub[c, f0 : f0 + nf, v].reshape(nf * modes, pts) for v in range(v0, v1)], axis=1
                )
                for c in range(2)
            ]
            w = wt[cut]
            if w.shape[0] < lanes:
                w = jnp.concatenate([w, jnp.zeros((lanes - w.shape[0], w.shape[1]), BF)], axis=0)
            full = mm(jnp.concatenate(u + [s_hi[cut]], axis=0), w, ((1,), (1,)))
            coef = fold(full[: 2 * nf * modes], nf, modes) * scale
            gram = fold(full[2 * nf * modes :], nf, blocks)
            coefs[g] = coef if ci == 0 else coefs[g] + coef
            grams[g] = gram if ci == 0 else grams[g] + gram
    width = tail_width(freqs, blocks, modes)
    per = modes // blocks
    tiles = [t for c in coefs for t in (c[i * blocks : (i + 1) * blocks] for i in range(per))]
    if width:
        lane = lax.broadcasted_iota(jnp.int32, (blocks, lanes), 1)
        tail = grams.pop()
        for i, t in enumerate(tiles[-per:]):
            tail = jnp.where(lane < (i + 1) * width, tail, pltpu.roll(t, (i + 1) * width, 1))
        tiles = tiles[:-per] + grams + [tail]
    else:
        tiles = tiles + grams
    for at, tile in enumerate(tiles):
        xb[at] = tile.astype(BF)

    pl.semaphore_wait(known.at[2], n_sp - 1)
    units = xb.shape[0]
    for t, s, first, size in owners:

        @pl.when((tm != t) | (sp != s))
        def _():
            pltpu.make_async_remote_copy(
                xb.at[pl.ds(first, size)], plane.at[here, pl.ds(0, size)], s1, r1,
                device_id={"tm": t, "space": s}, device_id_type=MESH,
            ).start()

    def wait_bytes(ref, sem):
        pltpu.make_async_copy(ref, ref, sem).wait()

    kinds_of = sorted({size for _, _, _, size in owners})
    holds = [
        (size, functools.reduce(jnp.logical_or, [m for m, o in zip(is_own, owners) if o[3] == size]))
        for size in kinds_of
    ]
    begin = sum(jnp.where(m, o[2], 0) for m, o in zip(is_own, owners))
    other = jnp.logical_not(functools.reduce(jnp.logical_or, is_own))
    for size, flag in holds:

        @pl.when(flag)
        def _():
            mine = pl.ds(begin, size)
            plane[here, 0:size] = xb[mine]
            wait_bytes(plane.at[pl.ds(0, side - 1), pl.ds(0, size)], r1)
            yb[mine] = jnp.sum(plane[:, 0:size].astype(F32), axis=0).astype(BF)

            def gather(i, carry):
                @pl.when(i != tm * n_sp + sp)
                def _():
                    pltpu.make_async_remote_copy(
                        yb.at[mine], yb.at[mine], s2, r2,
                        device_id={"tm": lax.div(i, n_sp), "space": lax.rem(i, n_sp)},
                        device_id_type=MESH,
                    ).start()

                return carry

            lax.fori_loop(0, side, gather, 0, unroll=side <= 32)
            wait_bytes(yb.at[pl.ds(0, units - size)], r2)

    @pl.when(other)
    def _():
        wait_bytes(yb, r2)

    y_out[...] = yb[...]
    for ci in range(len(chunks)):
        wait_bytes(recs[ci].at[pl.ds(0, n_tm - 1)], a_send.at[ci])
    for size, flag in holds:

        @pl.when(flag)
        def _():
            wait_bytes(xb.at[pl.ds(0, units - size)], s1)
            wait_bytes(plane.at[pl.ds(0, side - 1), pl.ds(0, size)], s2)

    @pl.when(other)
    def _():
        wait_bytes(xb, s1)


def finish(entries, yb, sh, coef_hbm, new_out, ob, coef_out, o_sem):
    freqs, nvar, modes, pts = new_out.shape[1:]
    blocks = coef_out.shape[1]
    lanes = yb.shape[2]
    groups = -(-freqs // GROUP)
    lane = lax.broadcasted_iota(jnp.int32, (modes, lanes), 1)
    lane_b = lane[:blocks]

    width = tail_width(freqs, blocks, modes)
    per = modes // blocks
    units = [yb[at].astype(F32) for at in range(yb.shape[0])]
    whole = groups - 1 if width else groups
    tiles = [jnp.concatenate(units[g * per : (g + 1) * per], axis=0) for g in range(whole)]
    grams = units[whole * per : whole * per + whole]
    if width:
        cuts = [pltpu.roll(units[-1], lanes - i * width, 1) if i else units[-1] for i in range(1 + per)]
        cuts = [jnp.where(lane_b < width, c, 0.0) for c in cuts]
        grams.append(cuts[0])
        tiles.append(jnp.concatenate(cuts[1:], axis=0))
    copies = []
    row_b = lax.broadcasted_iota(jnp.int32, (blocks, modes, lanes), 0)
    pick = row_b == lax.broadcasted_iota(jnp.int32, (blocks, modes, lanes), 2) % blocks
    picked = [
        jnp.where(pick, jnp.broadcast_to(t[None], pick.shape), 0.0).reshape(blocks * modes, lanes)
        for t in tiles
    ]
    lhs = jnp.concatenate(picked, axis=1).astype(BF)
    row = lax.broadcasted_iota(jnp.int32, (lanes, freqs), 0)
    col = lax.broadcasted_iota(jnp.int32, (lanes, freqs), 1)
    for c in range(2):
        moves = []
        for g in range(groups):
            half = min(GROUP, freqs - g * GROUP) * blocks
            hit = (row // half == c) & (col == row % half // blocks + g * GROUP)
            moves.append(jnp.where(hit, 1.0, 0.0).astype(BF))
        moved = mm(lhs, jnp.concatenate(moves, axis=0), ((1,), (0,)))
        coef_out[c] = moved.reshape(blocks, modes, freqs)
    cp = pltpu.make_async_copy(coef_out, coef_hbm, o_sem.at[groups])
    cp.start()
    copies.append(cp)

    for g in range(groups):
        f0 = g * GROUP
        nf = min(GROUP, freqs - f0)
        half = nf * blocks

        def spread(val):
            rows = val.shape[0]
            big = jnp.broadcast_to(val[None], (nf, rows, lanes))
            return jnp.where(freq_mask(nf, rows, lanes, blocks), big, 0.0).reshape(nf * rows, lanes)

        coef = tiles[g]
        gram = grams[g]
        vec = spread(jnp.where(lane < half, coef, -coef))
        turned = swap_halves(gram, half)
        quad = jnp.concatenate([spread(gram), spread(jnp.where(lane_b < half, -turned, turned))], axis=0)
        rows = [vec[:, : 2 * half].astype(BF), spread(swap_halves(coef, half))[:, : 2 * half].astype(BF)]
        energy = jnp.sum(vec * mm(rows[0], quad.astype(BF), ((1,), (0,))), axis=1, keepdims=True)
        factor = 1.0 / jnp.sqrt(energy / entries + 1e-06)
        both = jnp.concatenate(rows, axis=0)
        fields = mm(both, sh[g * lanes : g * lanes + 2 * half], ((1,), (0,)))
        for v in range(nvar):
            for c in range(2):
                val = (fields[c * nf * modes : (c + 1) * nf * modes, v * pts : (v + 1) * pts] * factor).astype(BF)
                ob[c, f0 : f0 + nf, v] = val.reshape(nf, modes, pts)
        cp = pltpu.make_async_copy(ob.at[:, pl.ds(f0, nf)], new_out.at[:, pl.ds(f0, nf)], o_sem.at[g])
        cp.start()
        copies.append(cp)

    for cp in copies:
        cp.wait()


def solution(mesh):
    n_tm, n_sp = mesh.shape["tm"], mesh.shape["space"]
    n = n_tm * n_sp

    def on_device(snapshots, basis, mass_table, elem_kind, offsets):
        rows, nvar, slab = snapshots.shape
        _, freqs, modes, _, pts = basis.shape
        blocks = offsets.shape[0]
        groups = -(-freqs // GROUP)
        entries = nvar * pts * n
        side = n_tm * n_sp
        units = unit_count(freqs, blocks, modes)
        owners = owner_list(n_tm, n_sp, units)
        table_rows = 2 * freqs * blocks
        unit = (blocks, 2 * GROUP * blocks)
        chunks = ((0, min(2, nvar)),) + tuple((v, v + 1) for v in range(2, nvar))
        snap = jnp.transpose(snapshots, (1, 0, 2))
        base = jnp.transpose(basis, (0, 1, 3, 2, 4))
        hbm = pl.BlockSpec(memory_space=pltpu.HBM)
        vmem = pl.BlockSpec(memory_space=pltpu.VMEM)
        spec, total = pl.pallas_call(
            functools.partial(kernel, n_tm, n_sp, owners, entries, chunks),
            out_shape=(
                jax.ShapeDtypeStruct((table_rows, nvar * pts), BF),
                jax.ShapeDtypeStruct((units,) + unit, BF),
            ),
            in_specs=[hbm] * 5,
            out_specs=(vmem, vmem),
            scratch_shapes=[
                pltpu.VMEM((table_rows, rows * n_tm), BF),
                pltpu.VMEM((2, freqs, nvar, modes, pts), BF),
                pltpu.VMEM((units,) + unit, BF),
                pltpu.VMEM((side, max(o[3] for o in owners)) + unit, BF),
                pltpu.VMEM((units,) + unit, BF),
                pltpu.VMEM(mass_table.shape, F32),
                pltpu.SMEM(elem_kind.shape, jnp.int32),
                pltpu.SMEM(offsets.shape, jnp.int32),
            ]
            + [pltpu.VMEM((n_tm, v1 - v0, rows, pts), BF) for v0, v1 in chunks]
            + [
                pltpu.SemaphoreType.DMA((len(chunks),)),
                pltpu.SemaphoreType.DMA((len(chunks),)),
                pltpu.SemaphoreType.DMA((4,)),
                pltpu.SemaphoreType.REGULAR((4,)),
            ]
            + [pltpu.SemaphoreType.DMA] * 4,
            compiler_params=pltpu.CompilerParams(
                collective_id=0, has_side_effects=True, vmem_limit_bytes=48 * 1024 * 1024
            ),
        )(*[pltpu.with_memory_space_constraint(a, pltpu.HBM) for a in (snap, base, mass_table, elem_kind, offsets)])
        coef, new = pl.pallas_call(
            functools.partial(finish, entries),
            out_shape=(
                jax.ShapeDtypeStruct((2, blocks, modes, freqs), F32),
                jax.ShapeDtypeStruct(base.shape, BF),
            ),
            in_specs=[vmem, vmem],
            out_specs=(hbm, hbm),
            scratch_shapes=[
                pltpu.VMEM(base.shape, BF),
                pltpu.VMEM((2, blocks, modes, freqs), F32),
                pltpu.SemaphoreType.DMA((groups + 1,)),
            ],
            compiler_params=pltpu.CompilerParams(vmem_limit_bytes=32 * 1024 * 1024),
        )(total, spec)
        return jnp.transpose(coef, (0, 3, 1, 2)), jnp.transpose(new, (0, 1, 3, 2, 4))

    return jax.shard_map(
        on_device,
        mesh=mesh,
        in_specs=(
            P("tm", None, "space"),
            P(None, None, None, None, ("space", "tm")),
            P(),
            P(("space", "tm")),
            P(),
        ),
        out_specs=(P(), P(None, None, None, None, ("space", "tm"))),
        check_vma=False,
    )
```

```python
import functools
import math

import jax
import jax.numpy as jnp
from jax import lax
from jax.experimental import pallas as pl
from jax.experimental.pallas import tpu as pltpu
from jax.sharding import PartitionSpec as P

NT = 256
GROUP = 8
LEVELS = 4
MESH = pl.DeviceIdType.MESH
BF = jnp.bfloat16
F32 = jnp.float32


def owner_list(n_tm, n_sp, units):
    quart = n_tm // LEVELS
    chips = [(quart, 0), (quart + 2, 0), (quart, n_sp - 1)]
    spots = [(t + c, s) for t, s in chips for c in range(2)]
    each, extra = divmod(units, len(spots))
    sizes = [each + (i < extra) for i in range(len(spots))]
    return tuple((t, s, sum(sizes[:i]), sizes[i]) for i, (t, s) in enumerate(spots))


def tail_width(freqs, blocks, modes):
    width = 2 * (freqs % GROUP) * blocks
    return width if 0 < width * (1 + modes // blocks) <= 2 * GROUP * blocks else 0


def unit_count(freqs, blocks, modes):
    groups = -(-freqs // GROUP)
    per = 1 + modes // blocks
    return groups * per - (per - 1 if tail_width(freqs, blocks, modes) else 0)


def mm(a, b, contract):
    return lax.dot_general(a, b, (contract, ((), ())), preferred_element_type=F32)


def swap_halves(x, half):
    lanes = x.shape[1]
    if 2 * half == lanes:
        return pltpu.roll(x, half, 1)
    lane = lax.broadcasted_iota(jnp.int32, x.shape, 1)
    return jnp.where(lane < half, pltpu.roll(x, lanes - half, 1), pltpu.roll(x, half, 1))


def freq_mask(nf, rows, lanes, blocks):
    row_f = lax.broadcasted_iota(jnp.int32, (nf, rows, lanes), 0)
    lane = lax.broadcasted_iota(jnp.int32, (nf, rows, lanes), 2)
    half = nf * blocks
    return (row_f == lane % half // blocks) & (lane < 2 * half)


def kernel(
    n_tm, n_sp, owners, entries, chunks,
    snap, basis, mass_in, kinds_in, offs_in,
    sh, yb,
    table, ub, xb, plane, mass, kinds, offs, *rest,
):
    recs, (a_send, a_recv, l_sem, known, s1, r1, s2, r2) = rest[: len(chunks)], rest[len(chunks) :]
    tm = lax.axis_index("tm")
    sp = lax.axis_index("space")
    side = n_tm * n_sp
    scale = 1.0 / math.sqrt(entries)
    here = sp * n_tm + tm
    is_own = [(tm == t) & (sp == s) for t, s, _, _ in owners]
    quart = n_tm // LEVELS
    lev, place = lax.div(tm, quart), lax.rem(tm, quart)
    edge = (lev == 0) | (lev == LEVELS - 1)
    inward = jnp.where(lev < LEVELS // 2, 1, -1)
    freqs = basis.shape[1]
    rows, pts = recs[0].shape[2:]
    groups = -(-freqs // GROUP)
    counts = [min(GROUP, freqs - g * GROUP) for g in range(groups)]
    record = n_tm * rows
    blocks = offs.shape[0]
    modes = basis.shape[3]
    lanes = 2 * GROUP * blocks

    barrier = pltpu.get_barrier_semaphore()

    def signal(sem, to_tm, to_sp):
        pl.semaphore_signal(
            sem, inc=1, device_id={"tm": to_tm, "space": to_sp}, device_id_type=MESH
        )

    for dl in (1, -1, 0):

        def greet(i, carry):
            to = (lev + dl) * quart + lax.rem(place + i, quart)
            signal(barrier, to, sp)
            return carry

        @pl.when((lev + dl >= 0) & (lev + dl < LEVELS) & ((dl != -1) | (lev <= LEVELS // 2)))
        def _():
            lax.fori_loop(1 if dl == 0 else 0, quart, greet, 0, unroll=side <= 32)

    def greet_side(i, carry):
        signal(barrier, tm, lax.rem(sp + i, n_sp))
        return carry

    lax.fori_loop(1, n_sp, greet_side, 0, unroll=side <= 32)
    loads = [
        pltpu.make_async_copy(offs_in, offs, l_sem.at[0]),
        pltpu.make_async_copy(kinds_in, kinds, l_sem.at[1]),
        pltpu.make_async_copy(mass_in, mass, l_sem.at[2]),
        pltpu.make_async_copy(basis, ub, l_sem.at[3]),
    ]
    for cp in loads:
        cp.start()
    near = jnp.where((lev == 0) | (lev >= LEVELS // 2), 2, 3)
    pl.semaphore_wait(barrier, near * quart - 1 + n_sp - 1)

    def relay(stage, ways=(1, -1)):
        for dl in ways:
            seen = lev - dl * (stage - 1)

            @pl.when((seen >= 0) & (seen < LEVELS) & (lev + dl >= 0) & (lev + dl < LEVELS))
            def _():
                signal(known.at[stage - 2], tm + dl * quart, sp)

    def learn(stage):
        for dl in (1, -1):

            @pl.when((lev + dl * stage >= 0) & (lev + dl * stage < LEVELS))
            def _():
                pl.semaphore_wait(known.at[stage - 2], 1)

    def send_level(ci, to_lev, first=0):
        v0, v1 = chunks[ci]

        def send(i, carry):
            to = to_lev * quart + (lax.rem(place + i, quart) if first else quart - 1 - i)
            pltpu.make_async_remote_copy(
                snap.at[pl.ds(v0, v1 - v0), :, pl.ds(pl.multiple_of(to * pts, pts), pts)],
                recs[ci].at[tm], a_send.at[ci], a_recv.at[ci],
                device_id={"tm": to, "space": sp}, device_id_type=MESH,
            ).start()
            return carry

        lax.fori_loop(first, quart, send, 0, unroll=side <= 32)

    turn = lev == LEVELS // 2
    pl.when(jnp.logical_not(turn))(lambda: relay(2))
    pl.when(lev > LEVELS // 2)(lambda: signal(known.at[3], tm - quart, sp))
    for ci, (v0, v1) in enumerate(chunks):
        mine = snap.at[pl.ds(v0, v1 - v0), :, pl.ds(pl.multiple_of(tm * pts, pts), pts)]
        if ci == 0:
            send_level(ci, lev + inward)
            pl.when(jnp.logical_not(edge | turn))(lambda: send_level(ci, lev - inward))
            send_level(ci, lev, 1)
            learn(2)
            pl.when(jnp.logical_not(turn))(lambda: relay(3))
            send_level(ci, lev + 2 * inward)

            @pl.when(turn)
            def _():
                pl.semaphore_wait(known.at[3], 1)
                relay(2)
                relay(3)
                send_level(ci, lev - inward)

            learn(3)
            pl.when(edge)(lambda: send_level(ci, lev + 3 * inward))

            def tell(i, carry):
                signal(known.at[2], tm, lax.rem(sp + i, n_sp))
                return carry

            lax.fori_loop(1, n_sp, tell, 0, unroll=side <= 32)
        else:
            pl.when(edge)(lambda: send_level(ci, lev + 3 * inward))
            send_level(ci, lev + 2 * inward)
            send_level(ci, lev + inward)
            pl.when(jnp.logical_not(edge))(lambda: send_level(ci, lev - inward))
            send_level(ci, lev, 1)
        pltpu.make_async_copy(mine, recs[ci].at[tm], a_recv.at[ci]).start()

    loads[0].wait()
    row = lax.broadcasted_iota(jnp.int32, (blocks, record), 0)
    lag = lax.broadcasted_iota(jnp.int32, (blocks, record), 1)
    for b in range(blocks):
        lag = jnp.where(row == b, lag - offs[b], lag)
    inside = (lag >= 0) & (lag < NT)
    theta = jnp.clip(lag, 0, NT - 1).astype(F32) * (2.0 * math.pi / NT)
    c1, s1v = jnp.cos(theta), jnp.sin(theta)
    win = jnp.where(inside, (0.5 - 0.5 * c1) * (1.0 / math.sqrt(0.375 * NT)), 0.0)
    cc, ss = win, jnp.zeros_like(win)
    for g, nf in enumerate(counts):
        parts = []
        for _ in range(nf):
            parts.append((cc, -ss))
            cc, ss = cc * c1 - ss * s1v, ss * c1 + cc * s1v
        table[g * lanes : g * lanes + 2 * nf * blocks] = jnp.concatenate(
            [p[c] for c in range(2) for p in parts], axis=0
        ).astype(BF)

    loads[1].wait()
    loads[2].wait()
    size = mass.shape[1]
    elems = pts // size
    strips = []
    for e in range(elems):
        kind = jnp.full((size, size), kinds[e], jnp.int32)
        blk = mass[0]
        for k in range(1, mass.shape[0]):
            blk = jnp.where(kind == k, mass[k], blk)
        zero = jnp.zeros_like(blk)
        strips.append(jnp.concatenate([blk if j == e else zero for j in range(elems)], axis=1))
    m_all = jnp.concatenate(strips, axis=0)
    m_hi = m_all.astype(BF)
    m_lo = (m_all - m_hi.astype(F32)).astype(BF)
    m_stack = jnp.concatenate([m_hi, m_hi, m_lo], axis=0)

    loads[3].wait()
    def fold(full, nf, rows):
        mask = freq_mask(nf, rows, lanes, blocks)
        real, imag = [
            jnp.sum(jnp.where(mask, part.reshape(nf, rows, lanes), 0.0), axis=0)
            for part in (full[: nf * rows], full[nf * rows :])
        ]
        imag = swap_halves(imag, nf * blocks)
        lane = lax.broadcasted_iota(jnp.int32, (rows, lanes), 1)
        return real + jnp.where(lane < nf * blocks, imag, -imag)

    coefs, grams = [None] * groups, [None] * groups
    for ci, (v0, v1) in enumerate(chunks):
        rec = recs[ci]
        pltpu.make_async_copy(rec, rec, a_recv.at[ci]).wait()
        count = v1 - v0
        x = jnp.concatenate([rec[:, v].reshape(record, pts) for v in range(count)], axis=1)
        cuts = [0, table.shape[0]] if count > 1 else [0, lanes, 2 * lanes, 3 * lanes, table.shape[0]]
        spec = jnp.concatenate([mm(table[i:j], x, ((1,), (0,))) for i, j in zip(cuts, cuts[1:])], axis=0)
        s_hi = spec.astype(BF)
        s_lo = (spec - s_hi.astype(F32)).astype(BF)
        sh[:, v0 * pts : v1 * pts] = s_hi
        wts = []
        for v in range(count):
            cut = slice(v * pts, (v + 1) * pts)
            lhs = jnp.concatenate([s_hi[:, cut], s_lo[:, cut], s_hi[:, cut]], axis=1)
            wts.append(
                jnp.concatenate(
                    [mm(lhs[i:j], m_stack, ((1,), (0,))).astype(BF) for i, j in zip(cuts, cuts[1:])], axis=0
                )
            )
        wt = jnp.concatenate(wts, axis=1)
        for g, nf in enumerate(counts):
            cut = slice(g * lanes, g * lanes + 2 * nf * blocks)
            f0 = g * GROUP
            u = [
                jnp.concatenate(
                    [ub[c, f0 : f0 + nf, v].reshape(nf * modes, pts) for v in range(v0, v1)], axis=1
                )
                for c in range(2)
            ]
            w = wt[cut]
            if w.shape[0] < lanes:
                w = jnp.concatenate([w, jnp.zeros((lanes - w.shape[0], w.shape[1]), BF)], axis=0)
            full = mm(jnp.concatenate(u + [s_hi[cut]], axis=0), w, ((1,), (1,)))
            coef = fold(full[: 2 * nf * modes], nf, modes) * scale
            gram = fold(full[2 * nf * modes :], nf, blocks)
            coefs[g] = coef if ci == 0 else coefs[g] + coef
            grams[g] = gram if ci == 0 else grams[g] + gram
    width = tail_width(freqs, blocks, modes)
    per = modes // blocks
    tiles = [t for c in coefs for t in (c[i * blocks : (i + 1) * blocks] for i in range(per))]
    if width:
        lane = lax.broadcasted_iota(jnp.int32, (blocks, lanes), 1)
        tail = grams.pop()
        for i, t in enumerate(tiles[-per:]):
            tail = jnp.where(lane < (i + 1) * width, tail, pltpu.roll(t, (i + 1) * width, 1))
        tiles = tiles[:-per] + grams + [tail]
    else:
        tiles = tiles + grams
    for at, tile in enumerate(tiles):
        xb[at] = tile.astype(BF)

    pl.semaphore_wait(known.at[2], n_sp - 1)
    units = xb.shape[0]
    for t, s, first, size in owners:

        @pl.when((tm != t) | (sp != s))
        def _():
            pltpu.make_async_remote_copy(
                xb.at[pl.ds(first, size)], plane.at[here, pl.ds(0, size)], s1, r1,
                device_id={"tm": t, "space": s}, device_id_type=MESH,
            ).start()

    def wait_bytes(ref, sem):
        pltpu.make_async_copy(ref, ref, sem).wait()

    kinds_of = sorted({size for _, _, _, size in owners})
    holds = [
        (size, functools.reduce(jnp.logical_or, [m for m, o in zip(is_own, owners) if o[3] == size]))
        for size in kinds_of
    ]
    begin = sum(jnp.where(m, o[2], 0) for m, o in zip(is_own, owners))
    other = jnp.logical_not(functools.reduce(jnp.logical_or, is_own))
    for size, flag in holds:

        @pl.when(flag)
        def _():
            mine = pl.ds(begin, size)
            plane[here, 0:size] = xb[mine]
            wait_bytes(plane.at[pl.ds(0, side - 1), pl.ds(0, size)], r1)
            yb[mine] = jnp.sum(plane[:, 0:size].astype(F32), axis=0).astype(BF)

            def gather(i, carry):
                @pl.when(i != tm * n_sp + sp)
                def _():
                    pltpu.make_async_remote_copy(
                        yb.at[mine], yb.at[mine], s2, r2,
                        device_id={"tm": lax.div(i, n_sp), "space": lax.rem(i, n_sp)},
                        device_id_type=MESH,
                    ).start()

                return carry

            lax.fori_loop(0, side, gather, 0, unroll=side <= 32)
            wait_bytes(yb.at[pl.ds(0, units - size)], r2)

    @pl.when(other)
    def _():
        wait_bytes(yb, r2)

    for ci in range(len(chunks)):
        wait_bytes(recs[ci].at[pl.ds(0, n_tm - 1)], a_send.at[ci])
    for size, flag in holds:

        @pl.when(flag)
        def _():
            wait_bytes(xb.at[pl.ds(0, units - size)], s1)
            wait_bytes(plane.at[pl.ds(0, side - 1), pl.ds(0, size)], s2)

    @pl.when(other)
    def _():
        wait_bytes(xb, s1)


def finish(entries, yb, sh, coef_hbm, new_out, ob, coef_out, o_sem):
    freqs, nvar, modes, pts = new_out.shape[1:]
    blocks = coef_out.shape[1]
    lanes = yb.shape[2]
    groups = -(-freqs // GROUP)
    lane = lax.broadcasted_iota(jnp.int32, (modes, lanes), 1)
    lane_b = lane[:blocks]

    width = tail_width(freqs, blocks, modes)
    per = modes // blocks
    units = [yb[at].astype(F32) for at in range(yb.shape[0])]
    whole = groups - 1 if width else groups
    tiles = [jnp.concatenate(units[g * per : (g + 1) * per], axis=0) for g in range(whole)]
    grams = units[whole * per : whole * per + whole]
    if width:
        cuts = [pltpu.roll(units[-1], lanes - i * width, 1) if i else units[-1] for i in range(1 + per)]
        cuts = [jnp.where(lane_b < width, c, 0.0) for c in cuts]
        grams.append(cuts[0])
        tiles.append(jnp.concatenate(cuts[1:], axis=0))
    copies = []
    row_b = lax.broadcasted_iota(jnp.int32, (blocks, modes, lanes), 0)
    pick = row_b == lax.broadcasted_iota(jnp.int32, (blocks, modes, lanes), 2) % blocks
    picked = [
        jnp.where(pick, jnp.broadcast_to(t[None], pick.shape), 0.0).reshape(blocks * modes, lanes)
        for t in tiles
    ]
    lhs = jnp.concatenate(picked, axis=1).astype(BF)
    row = lax.broadcasted_iota(jnp.int32, (lanes, freqs), 0)
    col = lax.broadcasted_iota(jnp.int32, (lanes, freqs), 1)
    for c in range(2):
        moves = []
        for g in range(groups):
            half = min(GROUP, freqs - g * GROUP) * blocks
            hit = (row // half == c) & (col == row % half // blocks + g * GROUP)
            moves.append(jnp.where(hit, 1.0, 0.0).astype(BF))
        moved = mm(lhs, jnp.concatenate(moves, axis=0), ((1,), (0,)))
        coef_out[c] = moved.reshape(blocks, modes, freqs)
    cp = pltpu.make_async_copy(coef_out, coef_hbm, o_sem.at[groups])
    cp.start()
    copies.append(cp)

    for g in range(groups):
        f0 = g * GROUP
        nf = min(GROUP, freqs - f0)
        half = nf * blocks

        def spread(val):
            rows = val.shape[0]
            big = jnp.broadcast_to(val[None], (nf, rows, lanes))
            return jnp.where(freq_mask(nf, rows, lanes, blocks), big, 0.0).reshape(nf * rows, lanes)

        coef = tiles[g]
        gram = grams[g]
        vec = spread(jnp.where(lane < half, coef, -coef))
        turned = swap_halves(gram, half)
        quad = jnp.concatenate([spread(gram), spread(jnp.where(lane_b < half, -turned, turned))], axis=0)
        rows = [vec[:, : 2 * half].astype(BF), spread(swap_halves(coef, half))[:, : 2 * half].astype(BF)]
        energy = jnp.sum(vec * mm(rows[0], quad.astype(BF), ((1,), (0,))), axis=1, keepdims=True)
        factor = 1.0 / jnp.sqrt(energy / entries + 1e-06)
        both = jnp.concatenate(rows, axis=0)
        fields = mm(both, sh[g * lanes : g * lanes + 2 * half], ((1,), (0,)))
        for v in range(nvar):
            for c in range(2):
                val = (fields[c * nf * modes : (c + 1) * nf * modes, v * pts : (v + 1) * pts] * factor).astype(BF)
                ob[c, f0 : f0 + nf, v] = val.reshape(nf, modes, pts)
        cp = pltpu.make_async_copy(ob.at[:, pl.ds(f0, nf)], new_out.at[:, pl.ds(f0, nf)], o_sem.at[g])
        cp.start()
        copies.append(cp)

    for cp in copies:
        cp.wait()


def solution(mesh):
    n_tm, n_sp = mesh.shape["tm"], mesh.shape["space"]
    n = n_tm * n_sp

    def on_device(snapshots, basis, mass_table, elem_kind, offsets):
        rows, nvar, slab = snapshots.shape
        _, freqs, modes, _, pts = basis.shape
        blocks = offsets.shape[0]
        groups = -(-freqs // GROUP)
        entries = nvar * pts * n
        side = n_tm * n_sp
        units = unit_count(freqs, blocks, modes)
        owners = owner_list(n_tm, n_sp, units)
        table_rows = 2 * freqs * blocks
        unit = (blocks, 2 * GROUP * blocks)
        chunks = ((0, min(2, nvar)),) + tuple((v, v + 1) for v in range(2, nvar))
        snap = jnp.transpose(snapshots, (1, 0, 2))
        base = jnp.transpose(basis, (0, 1, 3, 2, 4))
        hbm = pl.BlockSpec(memory_space=pltpu.HBM)
        vmem = pl.BlockSpec(memory_space=pltpu.VMEM)
        spec, total = pl.pallas_call(
            functools.partial(kernel, n_tm, n_sp, owners, entries, chunks),
            out_shape=(
                jax.ShapeDtypeStruct((table_rows, nvar * pts), BF),
                jax.ShapeDtypeStruct((units,) + unit, BF),
            ),
            in_specs=[hbm] * 5,
            out_specs=(vmem, vmem),
            scratch_shapes=[
                pltpu.VMEM((table_rows, rows * n_tm), BF),
                pltpu.VMEM((2, freqs, nvar, modes, pts), BF),
                pltpu.VMEM((units,) + unit, BF),
                pltpu.VMEM((side, max(o[3] for o in owners)) + unit, BF),
                pltpu.VMEM(mass_table.shape, F32),
                pltpu.SMEM(elem_kind.shape, jnp.int32),
                pltpu.SMEM(offsets.shape, jnp.int32),
            ]
            + [pltpu.VMEM((n_tm, v1 - v0, rows, pts), BF) for v0, v1 in chunks]
            + [
                pltpu.SemaphoreType.DMA((len(chunks),)),
                pltpu.SemaphoreType.DMA((len(chunks),)),
                pltpu.SemaphoreType.DMA((4,)),
                pltpu.SemaphoreType.REGULAR((4,)),
            ]
            + [pltpu.SemaphoreType.DMA] * 4,
            compiler_params=pltpu.CompilerParams(
                collective_id=0, has_side_effects=True, vmem_limit_bytes=48 * 1024 * 1024
            ),
        )(*[pltpu.with_memory_space_constraint(a, pltpu.HBM) for a in (snap, base, mass_table, elem_kind, offsets)])
        coef, new = pl.pallas_call(
            functools.partial(finish, entries),
            out_shape=(
                jax.ShapeDtypeStruct((2, blocks, modes, freqs), F32),
                jax.ShapeDtypeStruct(base.shape, BF),
            ),
            in_specs=[vmem, vmem],
            out_specs=(hbm, hbm),
            scratch_shapes=[
                pltpu.VMEM(base.shape, BF),
                pltpu.VMEM((2, blocks, modes, freqs), F32),
                pltpu.SemaphoreType.DMA((groups + 1,)),
            ],
            compiler_params=pltpu.CompilerParams(vmem_limit_bytes=32 * 1024 * 1024),
        )(total, spec)
        return jnp.transpose(coef, (0, 3, 1, 2)), jnp.transpose(new, (0, 1, 3, 2, 4))

    return jax.shard_map(
        on_device,
        mesh=mesh,
        in_specs=(
            P("tm", None, "space"),
            P(None, None, None, None, ("space", "tm")),
            P(),
            P(("space", "tm")),
            P(),
        ),
        out_specs=(P(), P(None, None, None, None, ("space", "tm"))),
        check_vma=False,
    )
```
